32 devices in a mesh: groups: 2 (over x), ep: 16 (over z, y, core).
Axes of the slice: x: 2, y: 2, z: 4, core: 2. Of those that a mesh axis runs over, the one named last changes fastest.
Arguments:
- thinker_rows: bfloat16 [512, 2048], P(('groups', 'ep')), parts along dimension 0, may hold values from -6 to 6
- expert_ids: int32 [512, 8], P(('groups', 'ep')), parts along dimension 0, may hold values from 0 to 15, all different within a row; in each aligned block of 16 rows (0 to 15, 16 to 31, ...) at most 16 rows name the same one
- gate_weights: float32 [512, 8], P(('groups', 'ep')), parts along dimension 0, may hold values from 0.2 to 1
- w_gate: bfloat16 [16, 2048, 512], P('ep'), may hold values from -0.125 to 0.125
- w_up: bfloat16 [16, 2048, 512], P('ep'), may hold values from -0.125 to 0.125
- w_down: bfloat16 [16, 512, 2048], P('ep'), may hold values from -0.25 to 0.25
- talker_proj: bfloat16 [2048, 1024], replicated, may hold values from -0.125 to 0.125
- talker_slot: int32 [32, 16], P(('groups', 'ep')), parts along dimension 0, may hold values from 0 to 15, each once within a row
- speech_count: int32 [512], P(('groups', 'ep')), parts along dimension 0, may hold values from 0 to 4
- left_context: bfloat16 [512, 6, 1024], P(('groups', 'ep')), parts along dimension 0, may hold values from -6 to 6
- frame_offset: float32 [4, 1024], replicated, may hold values from -6 to 6
- conv_weight: float32 [7, 1024], replicated, may hold values from -2.4 to 2.4
Outputs:
- voice_frames: bfloat16 [512, 4, 1024], P(('groups', 'ep')), parts along dimension 0
The draws below stay inside these ranges and needn't reach their ends.
There are 2 independent parts, one for each index of `groups`. The reference program is written for one: setup_inputs(seed, part) draws one part's arguments, and reference() takes and returns one part's arrays. A program takes and returns all parts, laid end to end along the dimension named above; an argument that names none is the same for every part. Nothing has to cross between parts.
Inputs may be any that keep to these rules, and one draw needn't show every extreme that they name: `expert_ids`: each row names 8 different experts; among the rows of one device no expert is named by more than 16 rows, and in every draw some expert is named by exactly 16 rows of some device. `talker_slot`: each device's row is a permutation of 0 to 15.
All inputs are finite; a program needn't handle non-finite values.
Results may differ from the reference program's by a relative error of at most 0.007.
Values may be sent and summed in bfloat16 or wider, within the bound.
No kernel may reach another device: no remote copies, remote signals or barrier semaphores. Data moves between devices by JAX's collectives and lax.ppermute only.
A program may use at most 64 MiB of HBM per device.

```python
import math
import jax
import jax.numpy as jnp
import numpy as np
from jax import lax

D = 2048
MOE_FF = 512
TD = 1024
TOPK = 8
KW = 7
FR = 4
HCAP = 1
EXPERTS = 16
OWNERS = 16
STR_DEV = 16
STREAMS = 256
CAP = 16


def place_ends(drawn, own_key, smallest, top_value):
    shape = drawn.shape
    spot = [jax.random.randint(jax.random.fold_in(own_key, axis), (), 0, shape[axis]) for axis in range(len(shape))]
    drawn = drawn.at[tuple(spot)].set(smallest)
    longest = shape.index(max(shape))
    spot[longest] = (spot[longest] + 1) % shape[longest]
    return drawn.at[tuple(spot)].set(top_value)


def levels(own_key, extent, cuts, low, largest):
    factor_of = 1.0
    for dim, parts in cuts:
        draws = jax.random.uniform(jax.random.fold_in(jax.random.fold_in(own_key, 6), dim), (parts,), jnp.float32, low / len(cuts), largest / len(cuts))
        factor_of = factor_of * jnp.repeat(jnp.exp(draws), extent[dim] // parts).reshape((-1,) + (1,) * (len(extent) - 1 - dim))
    return factor_of


def shared_out(stream_key, own, number, rows, number_of, top, limit, slope):
    order = jax.random.permutation(stream_key, number_of)
    crowded, common = shares(number_of, rows * top, limit, slope, True), shares(number_of, rows * top, limit, slope, False)
    places = jnp.arange(number_of)

    def named(sizes, offset_by):
        used = int((sizes > 0).sum())
        fixed = max(1, used // 4)
        moved = fixed + (places - fixed + offset_by * (used - fixed)) % max(1, number_of - fixed)
        return jnp.zeros((number_of,), jnp.int32).at[order[jnp.where(places < fixed, places, moved)]].set(jnp.asarray(sizes, jnp.int32))

    sizes = jnp.where(number % 4 == 0, named(crowded, number // 4), named(common, number - number // 4 - 1))
    mixed = jax.random.permutation(jax.random.fold_in(own, 3), number_of)
    source_of, receiver = mixed[0:number_of // 2 * 2:2], mixed[1:number_of // 2 * 2:2]
    room = jnp.minimum(sizes[source_of] - 1, limit - sizes[receiver]) // 2
    room = jnp.where((source_of == order[0]) | (receiver == order[0]) | (sizes[receiver] == 0), 0, jnp.maximum(room, 0))
    moved = jax.random.randint(jax.random.fold_in(own, 4), (number_of // 2,), 0, 1 << 20) % (room + 1)
    sizes = sizes.at[source_of].add(-moved).at[receiver].add(moved)
    items = jnp.searchsorted(jnp.cumsum(sizes), jnp.arange(rows * top), side="right").astype(jnp.int32)
    grid = items.reshape(top, rows).T
    grid = grid[jax.random.permutation(jax.random.fold_in(own, 1), rows)]
    offset_by = jax.random.randint(jax.random.fold_in(own, 2), (rows, 1), 0, top)
    return jnp.take_along_axis(grid, (jnp.arange(top)[None, :] + offset_by) % top, axis=1)


def shares(amount, total, bound, skew, full):
    loads = [(1 << 20) // math.isqrt(grade ** skew) + 1 for grade in range(1, amount + 1)]
    largest = bound if full else min(bound, max(-(-total // amount), total * loads[0] // sum(loads)))
    least = 1 if total - largest >= amount - 1 else 0
    holding, surplus = [largest] + [least] * (amount - 1), total - largest - least * (amount - 1)
    while surplus > 0:
        candidates = [i for i in range(1, amount) if holding[i] < largest] or [i for i in range(1, amount) if holding[i] < bound]
        pool, budget = sum([loads[i] for i in candidates]), surplus
        for i in candidates:
            extra = min(bound - holding[i], max(1, budget * loads[i] // pool), surplus)
            holding[i] = holding[i] + extra
            surplus = surplus - extra
    return np.array(holding)


def gaussian(key, shape, scale, reach, shards=(), kind=jnp.bfloat16):
    drawn = jax.random.normal(key, shape, jnp.float32) * scale
    if len(shards) > 0:
        drawn = levels(key, shape, shards, -0.22, 0.18) * drawn
    return jnp.clip(drawn, min=-reach, max=reach).astype(kind)


def setup_inputs(seed: int = 0, part: int = 0) -> dict:
    arg_keys = jax.random.split(jax.random.key(seed), 13)
    part_keys = jax.random.split(jax.random.fold_in(arg_keys[12], part), 13)
    thinker_rows = gaussian(part_keys[0], (STREAMS, D), 1.0, 6.0, ((0, 16),))
    expert_ids_keys = jax.random.split(jax.random.fold_in(part_keys[1], 1), STREAMS // STR_DEV)
    expert_ids_turns = jax.random.permutation(jax.random.fold_in(part_keys[1], 3), STREAMS // STR_DEV)
    expert_ids = jax.vmap(lambda own, number: shared_out(jax.random.fold_in(part_keys[1], 2), own, number, STR_DEV, EXPERTS, TOPK, CAP, 2))(expert_ids_keys, expert_ids_turns).reshape((STREAMS, TOPK))
    gate_weights = jnp.clip(jnp.exp(math.log(1.0) - 1.609438 * jax.random.uniform(part_keys[2], (STREAMS, TOPK), jnp.float32) ** levels(part_keys[2], (STREAMS, TOPK), ((0, 16),), -0.2, 0.2)), 0.2, 1.0)
    w_gate = gaussian(arg_keys[3], (EXPERTS, D, MOE_FF), D ** -0.5, 0.125, ((0, 16),))
    w_up = gaussian(arg_keys[4], (EXPERTS, D, MOE_FF), D ** -0.5, 0.125, ((0, 16),))
    w_down = gaussian(arg_keys[5], (EXPERTS, MOE_FF, D), MOE_FF ** -0.5, 0.25, ((0, 16),))
    talker_proj = gaussian(arg_keys[6], (D, TD), D ** -0.5, 0.125)
    talker_slot = jax.vmap(lambda own: jax.random.permutation(own, STR_DEV))(jax.random.split(part_keys[7], OWNERS)).reshape((OWNERS, STR_DEV)).astype(jnp.int32)
    speech_count = place_ends(jax.random.randint(part_keys[8], (STREAMS,), 0, FR + 1), jax.random.fold_in(part_keys[8], 1), 0, FR).astype(jnp.int32)
    left_context = gaussian(part_keys[9], (STREAMS, KW - 1, TD), 1.0, 6.0, ((0, 16),))
    frame_offset = gaussian(arg_keys[10], (FR, TD), 1.0, 6.0, (), jnp.float32)
    conv_weight = gaussian(arg_keys[11], (KW, TD), 0.4, 2.4, (), jnp.float32)
    return {"thinker_rows": thinker_rows, "expert_ids": expert_ids, "gate_weights": gate_weights, "w_gate": w_gate, "w_up": w_up, "w_down": w_down, "talker_proj": talker_proj, "talker_slot": talker_slot, "speech_count": speech_count, "left_context": left_context, "frame_offset": frame_offset, "conv_weight": conv_weight}


def expert_block(block_rows, gate_mat, up_mat, down_mat):
    gate_act = jnp.dot(block_rows, gate_mat, preferred_element_type=jnp.float32)
    up_act = jnp.dot(block_rows, up_mat, preferred_element_type=jnp.float32)
    inner = (jax.nn.silu(gate_act) * up_act).astype(jnp.bfloat16)
    return jnp.dot(inner, down_mat, preferred_element_type=jnp.float32).astype(jnp.bfloat16)

def project(hidden, talker_proj):
    values = hidden.astype(jnp.float32)
    scaled = values * lax.rsqrt(lax.optimization_barrier(jnp.mean(values * values, axis=-1, keepdims=True)) + 1e-06)
    return jnp.dot(scaled.astype(jnp.bfloat16), talker_proj, preferred_element_type=jnp.float32).astype(jnp.bfloat16)

def vocode(owned, speech_count, left_context, frame_offset, conv_weight):
    frames = owned.astype(jnp.float32)[:, None, :] + frame_offset[None, :, :]
    sequence = jnp.concatenate([left_context.astype(jnp.float32), frames], axis=1)
    taps = conv_weight.shape[0]
    horizon = frame_offset.shape[0]
    result = jnp.zeros_like(frames)
    for offset in range(taps):
        result = result + conv_weight[offset][None, None, :] * sequence[:, offset:offset + horizon, :]
    active = jnp.arange(horizon, dtype=jnp.int32)[None, :, None] < speech_count[:, None, None]
    return jnp.where(active, result, 0.0).astype(jnp.bfloat16)

def reference(thinker_rows, expert_ids, gate_weights, w_gate, w_up, w_down, talker_proj, talker_slot, speech_count, left_context, frame_offset, conv_weight):
    owners = STREAMS // STR_DEV
    blocks = expert_ids.reshape(owners, STR_DEV * TOPK)
    labels = jnp.arange(EXPERTS, dtype=jnp.int32)
    onehot = (blocks[:, :, None] == labels[None, None, :]).astype(jnp.int32)
    position = lax.optimization_barrier(jnp.sum((jnp.cumsum(onehot, axis=1) - onehot) * onehot, axis=2)).reshape(-1).astype(jnp.int32)
    flat_expert = expert_ids.reshape(-1).astype(jnp.int32)
    assigned = jnp.arange(STREAMS * TOPK, dtype=jnp.int32)
    source = assigned // (STR_DEV * TOPK)
    row_index = assigned // TOPK
    padded_rows = jnp.concatenate([thinker_rows, jnp.zeros((1, D), thinker_rows.dtype)], axis=0)

    def run_expert(expert):
        target = jnp.where(flat_expert == expert, source, owners)
        table = jnp.full((owners, CAP), STREAMS, jnp.int32).at[target, position].set(row_index, mode='drop')
        block_rows = padded_rows[table.reshape(-1)]
        return expert_block(block_rows, w_gate[expert], w_up[expert], w_down[expert])
    outputs = lax.map(run_expert, labels).reshape(EXPERTS * owners * CAP, D)
    lookup = (flat_expert * (owners * CAP) + source * CAP + position).reshape(STREAMS, TOPK)
    mixture = thinker_rows.astype(jnp.float32)
    for rank_index in range(TOPK):
        mixture = mixture + gate_weights[:, rank_index, None] * outputs[lookup[:, rank_index]].astype(jnp.float32)
    hidden = mixture.astype(jnp.bfloat16)
    talker_rows = project(hidden, talker_proj)
    slots = talker_slot.reshape(-1).astype(jnp.int32)
    stream_ids = jnp.arange(STREAMS, dtype=jnp.int32)
    owner_index = slots // HCAP * STR_DEV + stream_ids // STR_DEV * HCAP + slots % HCAP
    owned = jnp.zeros((STREAMS, TD), talker_rows.dtype).at[owner_index].set(talker_rows)
    return vocode(owned, speech_count, left_context, frame_offset, conv_weight)
```

```python
import functools

import jax
import jax.numpy as jnp
import numpy as np
from jax import lax
from jax.experimental import pallas as pl
from jax.experimental.pallas import tpu as pltpu
from jax.sharding import PartitionSpec as P

CAP = 16
LANES = 128


def expert_block(block_rows, gate_mat, up_mat, down_mat):
    gate_act = jnp.dot(block_rows, gate_mat, preferred_element_type=jnp.float32)
    up_act = jnp.dot(block_rows, up_mat, preferred_element_type=jnp.float32)
    inner = (jax.nn.silu(gate_act) * up_act).astype(jnp.bfloat16)
    return jnp.dot(inner, down_mat, preferred_element_type=jnp.float32).astype(jnp.bfloat16)


def project(hidden, talker_proj):
    values = hidden.astype(jnp.float32)
    scaled = values * lax.rsqrt(jnp.mean(values * values, axis=-1, keepdims=True) + 1e-06)
    return jnp.dot(
        scaled.astype(jnp.bfloat16), talker_proj, preferred_element_type=jnp.float32
    ).astype(jnp.bfloat16)


def vocode(owned, speech_count, left_context, frame_offset, conv_weight):
    frames = owned.astype(jnp.float32)[:, None, :] + frame_offset[None, :, :]
    sequence = jnp.concatenate([left_context.astype(jnp.float32), frames], axis=1)
    taps = conv_weight.shape[0]
    horizon = frame_offset.shape[0]
    result = jnp.zeros_like(frames)
    for offset in range(taps):
        result = (
            result + conv_weight[offset][None, None, :] * sequence[:, offset : offset + horizon, :]
        )
    active = jnp.arange(horizon, dtype=jnp.int32)[None, :, None] < speech_count[:, None, None]
    return jnp.where(active, result, 0.0).astype(jnp.bfloat16)


def slot_positions(expert_ids, experts):
    flat_expert = expert_ids.reshape(-1)
    onehot = (flat_expert[:, None] == jnp.arange(experts, dtype=jnp.int32)[None, :]).astype(
        jnp.int32
    )
    position = jnp.sum((jnp.cumsum(onehot, axis=0) - onehot) * onehot, axis=1)
    return (flat_expert, position)


def run_and_return(buffer, w_gate, w_up, w_down):
    sources, slot_count, features = buffer.shape
    flattened = buffer.reshape(sources * slot_count, features)
    outputs = expert_block(flattened, w_gate[0], w_up[0], w_down[0]).reshape(
        sources, slot_count, features
    )
    return lax.all_to_all(outputs, "ep", split_axis=0, concat_axis=0, tiled=True)


def local_dispatch(
    thinker_rows,
    expert_ids,
    gate_weights,
    w_gate,
    w_up,
    w_down,
    talker_proj,
    talker_slot,
    speech_count,
    left_context,
    frame_offset,
    conv_weight,
):
    devices = lax.axis_size("ep")
    streams_here, features = thinker_rows.shape
    chosen = expert_ids.shape[1]
    flat_expert, position = slot_positions(expert_ids, devices)
    row_index = jnp.arange(streams_here * chosen, dtype=jnp.int32) // chosen
    outgoing = (
        jnp.zeros((devices, CAP, features), jnp.bfloat16)
        .at[flat_expert, position]
        .set(thinker_rows[row_index])
    )
    returned = run_and_return(
        lax.all_to_all(outgoing, "ep", split_axis=0, concat_axis=0, tiled=True),
        w_gate,
        w_up,
        w_down,
    )
    lookup = (
        returned[flat_expert, position].astype(jnp.float32).reshape(streams_here, chosen, features)
    )
    mixture = jnp.sum(gate_weights[:, :, None] * lookup, axis=1)
    hidden = (thinker_rows.astype(jnp.float32) + mixture).astype(jnp.bfloat16)
    slots = talker_slot[0]
    per_owner = streams_here // devices
    talker_rows = project(hidden, talker_proj)
    placed = (
        jnp.zeros_like(talker_rows)
        .at[slots]
        .set(talker_rows)
        .reshape(devices, per_owner, talker_rows.shape[1])
    )
    owned = lax.all_to_all(placed, "ep", split_axis=0, concat_axis=0, tiled=True).reshape(
        streams_here, talker_rows.shape[1]
    )
    return vocode(owned, speech_count, left_context, frame_offset, conv_weight)


def dot32(a, b):
    return jnp.dot(a, b, preferred_element_type=jnp.float32)


def sort_kernel(experts, rows_ref, ids_ref, gates_ref, slot_ref, out_ref):
    rows, features = rows_ref.shape
    width = out_ref.shape[1] - features
    owner = lax.broadcasted_iota(jnp.int32, (rows, rows), 0)
    order = (owner == slot_ref[...]).astype(jnp.bfloat16)
    lane = lax.broadcasted_iota(jnp.int32, (rows, width), 1)
    expert = lane % experts
    gates = jnp.zeros((rows, width), jnp.float32)
    for j in range(ids_ref.shape[1]):
        gates = gates + jnp.where(expert == ids_ref[:, j : j + 1], gates_ref[:, j : j + 1], 0.0)
    high = gates.astype(jnp.bfloat16).astype(jnp.float32)
    middle = (gates - high).astype(jnp.bfloat16).astype(jnp.float32)
    low = gates - high - middle
    part = lane // experts
    packed = jnp.where(
        part == 0, high, jnp.where(part == 1, middle, jnp.where(part == 2, low, 0.0))
    ).astype(jnp.bfloat16)
    out_ref[:, :features] = dot32(order, rows_ref[...]).astype(jnp.bfloat16)
    out_ref[:, features:] = dot32(order, packed).astype(jnp.bfloat16)


def expert_kernel(
    blocks, move_ref, pick_ref, wg_ref, wu_ref, wd_ref, *refs
):
    parts, outs, x_ref, inner_ref = refs[:blocks], refs[blocks:-2], refs[-2], refs[-1]
    features = wg_ref.shape[0]
    hidden = wg_ref.shape[1]
    at = 0
    for part in parts:
        x_ref[at : at + part.shape[0], :] = part[...]
        at += part.shape[0]
    meta = x_ref[:, features:].astype(jnp.float32)
    gate = jnp.sum(meta * pick_ref[...], axis=1, keepdims=True)
    step = min(256, hidden)
    for n in range(0, hidden, step):
        g = dot32(x_ref[:, :features], wg_ref[:, n : n + step])
        u = dot32(x_ref[:, :features], wu_ref[:, n : n + step])
        inner_ref[:, n : n + step] = (g * jax.nn.sigmoid(g) * u * gate).astype(jnp.bfloat16)
    placed = dot32(move_ref[...], inner_ref[...]).astype(jnp.bfloat16)
    step = min(512, features)
    for n in range(0, features, step):
        y = dot32(placed, wd_ref[:, n : n + step]).astype(jnp.bfloat16)
        at = 0
        for out in outs:
            out[:, n : n + step] = y[at : at + out.shape[0]]
            at += out.shape[0]


def residual_kernel(blocks, pick_ref, *refs):
    parts, out_ref, x_ref = refs[:blocks], refs[-2], refs[-1]
    at = 0
    features = out_ref.shape[1]
    for part in parts:
        x_ref[at : at + part.shape[0], :] = part[:, :features]
        at += part.shape[0]
    out_ref[...] = dot32(pick_ref[...], x_ref[...]).astype(jnp.bfloat16)


def owner_kernel(mine_ref, got_ref, rest_ref, order_ref, proj_ref, base_ref, scale_ref, out_ref):
    total = mine_ref[...] + got_ref[...].astype(jnp.float32) + rest_ref[...].astype(jnp.float32)
    values = total.astype(jnp.bfloat16).astype(jnp.float32)
    normed = values * lax.rsqrt(jnp.mean(values * values, axis=-1, keepdims=True) + 1e-06)
    talker = dot32(normed.astype(jnp.bfloat16), proj_ref[...]).astype(jnp.bfloat16)
    owned = dot32(order_ref[...], talker)
    for q in range(owned.shape[0]):
        out_ref[q] = (base_ref[q] + scale_ref[q] * owned[q : q + 1, :]).astype(jnp.bfloat16)


def vmem(count):
    return [pl.BlockSpec(memory_space=pltpu.VMEM)] * count


def partner_lists(chips):
    masks = sorted(range(1, chips), key=lambda m: (-bin(m).count("1"), -m))
    return [masks[1::2], masks[0::2]]


def conv_parts(speech_count, left_context, frame_offset, conv_weight):
    taps, (horizon, past) = conv_weight.shape[0], (frame_offset.shape[0], left_context.shape[1])
    context = left_context.astype(jnp.float32)
    base, scale = [], []
    for f in range(horizon):
        b = jnp.zeros_like(context[:, 0, :])
        s = jnp.zeros_like(conv_weight[0])
        for t in range(taps):
            if f + t < past:
                b = b + conv_weight[t][None, :] * context[:, f + t, :]
            else:
                b = b + (conv_weight[t] * frame_offset[f + t - past])[None, :]
                s = s + conv_weight[t]
        base.append(b)
        scale.append(jnp.broadcast_to(s[None, :], b.shape))
    active = jnp.arange(horizon, dtype=jnp.int32)[None, :, None] < speech_count[:, None, None]
    base = jnp.where(active, jnp.stack(base, axis=1), 0.0)
    return base, jnp.where(active, jnp.stack(scale, axis=1), 0.0)


def local_gather(
    thinker_rows,
    expert_ids,
    gate_weights,
    w_gate,
    w_up,
    w_down,
    talker_proj,
    talker_slot,
    speech_count,
    left_context,
    frame_offset,
    conv_weight,
):
    devices = lax.axis_size("ep")
    rows, features = thinker_rows.shape
    talker_width = talker_proj.shape[1]
    horizon = frame_offset.shape[0]
    me = lax.axis_index("ep").astype(jnp.int32)
    core = me % 2
    lists = partner_lists(devices // 2)
    slots = max(len(lists[0]), len(lists[1]))
    width = -(-3 * devices // LANES) * LANES
    everyone = [(i, i ^ 1) for i in range(devices)]

    def far(x, j):
        pairs = [(i, i ^ (lists[i % 2][j] * 2)) for i in range(devices) if j < len(lists[i % 2])]
        return lax.ppermute(x, "ep", pairs)

    def near(x, j=None):
        pairs = [p for p in everyone if j is None or j < len(lists[p[0] % 2])]
        return lax.ppermute(x, "ep", pairs)

    def padded(values):
        return list(values) + [None] * (slots - len(values))

    def tables(c):
        origin = [0, 1]
        for flip, chips in ((0, padded(lists[c])), (1, padded(lists[1 - c]))):
            for m in chips:
                origin += [-1, -1] if m is None else [2 * m + flip, 2 * m + 1 - flip]
        target = []
        for flip, chips in ((0, padded(lists[c])), (1, padded(lists[1 - c]))):
            for m in chips:
                target += [-1, -1] if m is None else [2 * m + flip, 2 * m + 1 - flip]
        return np.array(origin, np.int32), np.array(target + [0, 1], np.int32)

    both = [tables(0), tables(1)]
    origin = jnp.where(core == 0, both[0][0], both[1][0])
    target = jnp.where(core == 0, both[0][1], both[1][1])
    r = jnp.arange(rows, dtype=jnp.int32)
    col_origin, col_owner = jnp.repeat(origin, rows), jnp.tile(r, origin.shape[0])
    row_target, row_rank = jnp.repeat(target, rows), jnp.tile(r, target.shape[0])
    move = (
        (row_target >= 0)[:, None]
        & (col_origin[None, :] == (row_target ^ row_rank)[:, None])
        & (col_owner[None, :] == (row_target ^ me)[:, None])
    ).astype(jnp.bfloat16)
    rest = ((col_origin[None, :] == r[:, None]) & (col_owner == me)[None, :]).astype(jnp.bfloat16)
    lane = jnp.arange(width, dtype=jnp.int32)
    pick = ((lane % devices == me) & (lane < 3 * devices)).astype(jnp.float32)[None, :]
    order = ((r[:, None] ^ r[None, :]) == me).astype(jnp.bfloat16)

    own = pl.pallas_call(
        functools.partial(sort_kernel, devices),
        out_shape=jax.ShapeDtypeStruct((rows, features + width), jnp.bfloat16),
        in_specs=vmem(4),
        out_specs=vmem(1)[0],
        name="sort_rows",
    )(thinker_rows, expert_ids, gate_weights, talker_slot)
    other = near(own)
    pair = jnp.concatenate([own, other])
    mine = [far(pair, j) for j in range(slots)]
    theirs = [near(mine[j], j) for j in range(slots)]
    parts = [pair] + mine + theirs
    total = sum(p.shape[0] for p in parts)

    keep, give, here = pl.pallas_call(
        functools.partial(expert_kernel, len(parts)),
        out_shape=[
            jax.ShapeDtypeStruct((2 * slots * rows, features), jnp.bfloat16),
            jax.ShapeDtypeStruct((2 * slots * rows, features), jnp.bfloat16),
            jax.ShapeDtypeStruct((2 * rows, features), jnp.bfloat16),
        ],
        in_specs=vmem(5 + len(parts)),
        out_specs=vmem(3),
        scratch_shapes=[
            pltpu.VMEM((total, features + width), jnp.bfloat16),
            pltpu.VMEM((total, w_gate.shape[2]), jnp.bfloat16),
        ],
        name="expert",
    )(move, pick, w_gate[0], w_up[0], w_down[0], *parts)

    residual = pl.pallas_call(
        functools.partial(residual_kernel, len(parts)),
        out_shape=jax.ShapeDtypeStruct((rows, features), jnp.bfloat16),
        in_specs=vmem(1 + len(parts)),
        out_specs=vmem(1)[0],
        scratch_shapes=[pltpu.VMEM((total, features), jnp.bfloat16)],
        name="residual",
    )(rest, *parts)

    given = near(give)
    chip_sum = (keep.astype(jnp.float32) + given.astype(jnp.float32)).astype(jnp.bfloat16)
    arrived = [far(chip_sum[2 * rows * j : 2 * rows * (j + 1)], j) for j in range(slots)]
    partial = here.astype(jnp.float32)
    for a in arrived:
        partial = partial + a.astype(jnp.float32)
    got = near(partial[rows:].astype(jnp.bfloat16))
    base, scale = conv_parts(speech_count, left_context, frame_offset, conv_weight)
    return pl.pallas_call(
        owner_kernel,
        out_shape=jax.ShapeDtypeStruct((rows, horizon, talker_width), jnp.bfloat16),
        in_specs=vmem(7),
        out_specs=vmem(1)[0],
        name="owner",
    )(partial[:rows], got, residual, order, talker_proj, base, scale)


def local(thinker_rows, *rest):
    devices = lax.axis_size("ep")
    rows = thinker_rows.shape[0]
    small = rows <= CAP and rows == devices and devices % 4 == 0 and devices & (devices - 1) == 0
    return (local_gather if small else local_dispatch)(thinker_rows, *rest)


def solution(mesh):
    in_specs = (
        P(("groups", "ep"), None),
        P(("groups", "ep"), None),
        P(("groups", "ep"), None),
        P("ep", None, None),
        P("ep", None, None),
        P("ep", None, None),
        P(),
        P(("groups", "ep"), None),
        P(("groups", "ep")),
        P(("groups", "ep"), None, None),
        P(),
        P(),
    )
    out_specs = P(("groups", "ep"), None, None)
    return jax.shard_map(local, mesh=mesh, in_specs=in_specs, out_specs=out_specs, check_vma=False)
```

```python
import functools

import jax
import jax.numpy as jnp
import numpy as np
from jax import lax
from jax.experimental import pallas as pl
from jax.experimental.pallas import tpu as pltpu
from jax.sharding import PartitionSpec as P

CAP = 16
LANES = 128


def expert_block(block_rows, gate_mat, up_mat, down_mat):
    gate_act = jnp.dot(block_rows, gate_mat, preferred_element_type=jnp.float32)
    up_act = jnp.dot(block_rows, up_mat, preferred_element_type=jnp.float32)
    inner = (jax.nn.silu(gate_act) * up_act).astype(jnp.bfloat16)
    return jnp.dot(inner, down_mat, preferred_element_type=jnp.float32).astype(jnp.bfloat16)


def project(hidden, talker_proj):
    values = hidden.astype(jnp.float32)
    scaled = values * lax.rsqrt(jnp.mean(values * values, axis=-1, keepdims=True) + 1e-06)
    return jnp.dot(
        scaled.astype(jnp.bfloat16), talker_proj, preferred_element_type=jnp.float32
    ).astype(jnp.bfloat16)


def vocode(owned, speech_count, left_context, frame_offset, conv_weight):
    frames = owned.astype(jnp.float32)[:, None, :] + frame_offset[None, :, :]
    sequence = jnp.concatenate([left_context.astype(jnp.float32), frames], axis=1)
    taps = conv_weight.shape[0]
    horizon = frame_offset.shape[0]
    result = jnp.zeros_like(frames)
    for offset in range(taps):
        result = (
            result + conv_weight[offset][None, None, :] * sequence[:, offset : offset + horizon, :]
        )
    active = jnp.arange(horizon, dtype=jnp.int32)[None, :, None] < speech_count[:, None, None]
    return jnp.where(active, result, 0.0).astype(jnp.bfloat16)


def slot_positions(expert_ids, experts):
    flat_expert = expert_ids.reshape(-1)
    onehot = (flat_expert[:, None] == jnp.arange(experts, dtype=jnp.int32)[None, :]).astype(
        jnp.int32
    )
    position = jnp.sum((jnp.cumsum(onehot, axis=0) - onehot) * onehot, axis=1)
    return (flat_expert, position)


def run_and_return(buffer, w_gate, w_up, w_down):
    sources, slot_count, features = buffer.shape
    flattened = buffer.reshape(sources * slot_count, features)
    outputs = expert_block(flattened, w_gate[0], w_up[0], w_down[0]).reshape(
        sources, slot_count, features
    )
    return lax.all_to_all(outputs, "ep", split_axis=0, concat_axis=0, tiled=True)


def local_dispatch(
    thinker_rows,
    expert_ids,
    gate_weights,
    w_gate,
    w_up,
    w_down,
    talker_proj,
    talker_slot,
    speech_count,
    left_context,
    frame_offset,
    conv_weight,
):
    devices = lax.axis_size("ep")
    streams_here, features = thinker_rows.shape
    chosen = expert_ids.shape[1]
    flat_expert, position = slot_positions(expert_ids, devices)
    row_index = jnp.arange(streams_here * chosen, dtype=jnp.int32) // chosen
    outgoing = (
        jnp.zeros((devices, CAP, features), jnp.bfloat16)
        .at[flat_expert, position]
        .set(thinker_rows[row_index])
    )
    returned = run_and_return(
        lax.all_to_all(outgoing, "ep", split_axis=0, concat_axis=0, tiled=True),
        w_gate,
        w_up,
        w_down,
    )
    lookup = (
        returned[flat_expert, position].astype(jnp.float32).reshape(streams_here, chosen, features)
    )
    mixture = jnp.sum(gate_weights[:, :, None] * lookup, axis=1)
    hidden = (thinker_rows.astype(jnp.float32) + mixture).astype(jnp.bfloat16)
    slots = talker_slot[0]
    per_owner = streams_here // devices
    talker_rows = project(hidden, talker_proj)
    placed = (
        jnp.zeros_like(talker_rows)
        .at[slots]
        .set(talker_rows)
        .reshape(devices, per_owner, talker_rows.shape[1])
    )
    owned = lax.all_to_all(placed, "ep", split_axis=0, concat_axis=0, tiled=True).reshape(
        streams_here, talker_rows.shape[1]
    )
    return vocode(owned, speech_count, left_context, frame_offset, conv_weight)


def dot32(a, b):
    return jnp.dot(a, b, preferred_element_type=jnp.float32)


def sort_rows(experts, rows_ref, ids_ref, gates_ref, slot_ref, out_ref, at):
    rows, features = rows_ref.shape
    width = out_ref.shape[1] - features
    owner = lax.broadcasted_iota(jnp.int32, (rows, rows), 0)
    order = (owner == slot_ref[...]).astype(jnp.bfloat16)
    lane = lax.broadcasted_iota(jnp.int32, (width, rows), 0)
    expert = lane % experts
    gates = jnp.zeros((width, rows), jnp.float32)
    for j in range(ids_ref.shape[0]):
        gates = gates + jnp.where(expert == ids_ref[j : j + 1, :], gates_ref[j : j + 1, :], 0.0)
    high = gates.astype(jnp.bfloat16).astype(jnp.float32)
    middle = (gates - high).astype(jnp.bfloat16).astype(jnp.float32)
    low = gates - high - middle
    part = lane // experts
    packed = jnp.where(
        part == 0, high, jnp.where(part == 1, middle, jnp.where(part == 2, low, 0.0))
    ).astype(jnp.bfloat16)
    out_ref[at : at + rows, :features] = dot32(order, rows_ref[...]).astype(jnp.bfloat16)
    out_ref[at : at + rows, features:] = lax.dot_general(
        order, packed, (((1,), (1,)), ((), ())), preferred_element_type=jnp.float32
    ).astype(jnp.bfloat16)


def own_kernel(experts, rows_ref, ids_ref, gates_ref, slot_ref, out_ref):
    sort_rows(experts, rows_ref, ids_ref, gates_ref, slot_ref, out_ref, 0)


def pair_kernel(own_ref, other_ref, out_ref):
    rows = own_ref.shape[0]
    out_ref[:rows, :] = own_ref[...]
    out_ref[rows:, :] = other_ref[...]


def fetch_kernel(*refs):
    count = (len(refs) - 1) // 2
    sems = refs[-1]
    copies = [
        pltpu.make_async_copy(refs[i], refs[count + i], sems.at[i]) for i in range(count)
    ]
    for copy in copies:
        copy.start()
    for copy in copies:
        copy.wait()


def move_rows(me, rows, table_ref, target_ref):
    core = me % 2
    columns = table_ref.shape[1]
    origin = jnp.where(core == 0, table_ref[0:1, :], table_ref[1:2, :])
    owner = lax.broadcasted_iota(jnp.int32, (1, columns), 1) % rows
    target = jnp.where(core == 0, target_ref[:, 0:1], target_ref[:, 1:2])
    rank = lax.broadcasted_iota(jnp.int32, target.shape, 0) % rows
    hit = (origin == (target ^ rank)) & (owner == (target ^ me)) & (target >= 0)
    return jnp.where(hit, 1.0, 0.0).astype(jnp.bfloat16)


def expert_kernel(blocks, experts, rows, table_ref, target_ref, wg_ref, wu_ref, wd_ref, *refs):
    parts, (out_ref, inner_ref, x_ref) = refs[:blocks], refs[blocks:]
    me = lax.axis_index("ep")
    features, hidden = wg_ref.shape
    at = 0
    for part in parts:
        x_ref[at : at + part.shape[0], :] = part[...]
        at += part.shape[0]
    meta = x_ref[:, features:].astype(jnp.float32)
    lane = lax.broadcasted_iota(jnp.int32, (1, meta.shape[1]), 1)
    pick = (lane % experts == me) & (lane < 3 * experts)
    gate = jnp.sum(jnp.where(pick, meta, 0.0), axis=1, keepdims=True)
    step = min(256, hidden)
    for n in range(0, hidden, step):
        g = dot32(x_ref[:, :features], wg_ref[:, n : n + step])
        u = dot32(x_ref[:, :features], wu_ref[:, n : n + step])
        inner_ref[:, n : n + step] = (g * jax.nn.sigmoid(g) * u * gate).astype(jnp.bfloat16)
    down(rows, table_ref, target_ref, wd_ref, inner_ref, out_ref)


def down(rows, table_ref, target_ref, wd_ref, inner_ref, out_ref):
    me = lax.axis_index("ep")
    move = move_rows(me, rows, table_ref, target_ref)
    placed = dot32(move, inner_ref[...]).astype(jnp.bfloat16)
    features = wd_ref.shape[1]
    step = min(512, features)
    for n in range(0, features, step):
        out_ref[:, n : n + step] = dot32(placed, wd_ref[:, n : n + step]).astype(jnp.bfloat16)


def prepare_kernel(blocks, rows, table_ref, context_ref, offset_ref, conv_ref, *refs):
    parts, (rest_ref, base_ref, x_ref) = refs[:blocks], refs[blocks:]
    me = lax.axis_index("ep")
    features = rest_ref.shape[1]
    at = 0
    for part in parts:
        x_ref[at : at + part.shape[0], :] = part[:, :features]
        at += part.shape[0]
    columns = table_ref.shape[1]
    origin = jnp.where(me % 2 == 0, table_ref[0:1, :], table_ref[1:2, :])
    owner = lax.broadcasted_iota(jnp.int32, (1, columns), 1) % rows
    rank = lax.broadcasted_iota(jnp.int32, (rows, 1), 0)
    pick = jnp.where((origin == rank) & (owner == me), 1.0, 0.0).astype(jnp.bfloat16)
    rest_ref[...] = dot32(pick, x_ref[...]).astype(jnp.bfloat16)
    taps, horizon, past = conv_ref.shape[0], offset_ref.shape[0], context_ref.shape[0]
    context = [context_ref[i].astype(jnp.float32) for i in range(past)]
    for f in range(horizon):
        fixed = jnp.zeros((1, conv_ref.shape[1]), jnp.float32)
        for t in range(past - f, taps):
            i = f + t - past
            fixed = fixed + conv_ref[t : t + 1, :] * offset_ref[i : i + 1, :]
        total = jnp.broadcast_to(fixed, context[0].shape)
        for t in range(past - f):
            total = total + conv_ref[t : t + 1, :] * context[f + t]
        base_ref[:, f, :] = total


def owner_kernel(
    count_ref, mine_ref, got_ref, rest_ref, proj_ref, base_ref, conv_ref, out_ref
):
    me = lax.axis_index("ep")
    rows = rest_ref.shape[0]
    total = mine_ref[:rows, :] + got_ref[...].astype(jnp.float32)
    total = total + rest_ref[...].astype(jnp.float32)
    values = total.astype(jnp.bfloat16).astype(jnp.float32)
    normed = values * lax.rsqrt(jnp.mean(values * values, axis=-1, keepdims=True) + 1e-06)
    talker = dot32(normed.astype(jnp.bfloat16), proj_ref[...]).astype(jnp.bfloat16)
    one = lax.broadcasted_iota(jnp.int32, (rows, rows), 0)
    two = lax.broadcasted_iota(jnp.int32, (rows, rows), 1)
    order = jnp.where((one ^ two) == me, 1.0, 0.0).astype(jnp.bfloat16)
    owned = dot32(order, talker)
    taps, horizon = conv_ref.shape[0], base_ref.shape[1]
    frame = lax.broadcasted_iota(jnp.int32, (horizon, owned.shape[1]), 0)
    scale = jnp.zeros(frame.shape, jnp.float32)
    for t in range(taps):
        scale = scale + jnp.where(frame + t >= taps - 1, conv_ref[t : t + 1, :], 0.0)
    for q in range(rows):
        voice = base_ref[q] + scale * owned[q : q + 1, :]
        out_ref[q] = jnp.where(frame < count_ref[q], voice, 0.0).astype(jnp.bfloat16)


def vmem(count):
    return [pl.BlockSpec(memory_space=pltpu.VMEM)] * count


def partner_lists(chips):
    masks = sorted(range(1, chips), key=lambda m: (-bin(m).count("1"), -m))
    return [masks[1::2] + [None], masks[0::2]]


def in_hbm(x):
    return pltpu.with_memory_space_constraint(x, pltpu.HBM)


def call(kernel, name, out_shape, operands, scalars=0, scratch=(), megabytes=4, cost=None, in_specs=None):
    several = isinstance(out_shape, (list, tuple))
    specs = [pl.BlockSpec(memory_space=pltpu.SMEM)] * scalars + vmem(len(operands) - scalars)
    return pl.pallas_call(
        kernel,
        out_shape=out_shape,
        in_specs=in_specs or specs,
        out_specs=vmem(len(out_shape)) if several else vmem(1)[0],
        scratch_shapes=list(scratch),
        compiler_params=pltpu.CompilerParams(vmem_limit_bytes=megabytes << 20),
        cost_estimate=cost,
        name=name,
    )(*operands)


def local_gather(
    thinker_rows,
    expert_ids,
    gate_weights,
    w_gate,
    w_up,
    w_down,
    talker_proj,
    talker_slot,
    speech_count,
    left_context,
    frame_offset,
    conv_weight,
):
    devices = lax.axis_size("ep")
    rows, features = thinker_rows.shape
    hidden = w_gate.shape[2]
    talker_width = talker_proj.shape[1]
    horizon = frame_offset.shape[0]
    lists = partner_lists(devices // 2)
    back = partner_lists(devices // 2)
    slots = len(lists[0])
    width = -(-3 * devices // LANES) * LANES
    bf16 = functools.partial(jax.ShapeDtypeStruct, dtype=jnp.bfloat16)

    def far(x, chips, j):
        pairs = [(i, i ^ (chips[i % 2][j] * 2)) for i in range(devices) if chips[i % 2][j]]
        return lax.ppermute(x, "ep", pairs)

    def near(x, j=None):
        pairs = [(i, i ^ 1) for i in range(devices) if j is None or lists[i % 2][j]]
        return lax.ppermute(x, "ep", pairs)

    def side(chips, flip):
        blocks = [[-1, -1] if m is None else [2 * m + flip, 2 * m + 1 - flip] for m in chips]
        return [k for pair in blocks for k in pair]

    def spread(blocks):
        return np.repeat(np.array(blocks, np.int32), rows)

    table = np.stack([spread([0, 1] + side(lists[c], 0) + side(lists[1 - c], 1)) for c in range(2)])
    keep_to = np.stack([spread(side(back[c], 0) + [0, 1]) for c in range(2)], axis=1)
    give_to = np.stack([spread(side(back[1 - c], 1)) for c in range(2)], axis=1)

    own = call(
        functools.partial(own_kernel, devices),
        "own_rows",
        bf16((rows, features + width)),
        [in_hbm(v) for v in (thinker_rows, expert_ids.T, gate_weights.T, talker_slot)],
        megabytes=4,
    )
    pair = call(pair_kernel, "pair_rows", bf16((2 * rows, features + width)), [own, near(own)])
    pair, w_up, w_down = lax.optimization_barrier((pair, w_up, w_down))
    mine = [far(pair, lists, j) for j in range(slots)]
    w_up_here, w_down_here = call(
        fetch_kernel,
        "fetch",
        [bf16(w_up.shape[1:]), bf16(w_down.shape[1:])],
        [in_hbm(w_up[0]), in_hbm(w_down[0])],
        in_specs=[pl.BlockSpec(memory_space=pltpu.HBM)] * 2,
        scratch=[pltpu.SemaphoreType.DMA((2,))],
        cost=pl.CostEstimate(flops=0, bytes_accessed=2 * w_up.size * 2, transcendentals=0),
    )
    mine[0], w_up_here, w_down_here = lax.optimization_barrier((mine[0], w_up_here, w_down_here))
    theirs = [near(mine[j], j) for j in range(slots)]
    parts = [pair] + mine + theirs
    total = sum(p.shape[0] for p in parts)
    give, inner = call(
        functools.partial(expert_kernel, len(parts), devices, rows),
        "expert",
        [bf16((2 * slots * rows, features)), bf16((total, hidden))],
        [table, give_to, w_gate[0], w_up_here, w_down_here] + parts,
        scratch=[pltpu.VMEM((total, features + width), jnp.bfloat16)],
        megabytes=12,
    )
    given = near(give)
    keep = call(
        functools.partial(down, rows),
        "expert_keep",
        bf16((2 * (slots + 1) * rows, features)),
        [table, keep_to, w_down_here, inner],
        megabytes=6,
        cost=pl.CostEstimate(
            flops=4 * (slots + 1) * rows * features * hidden,
            bytes_accessed=2 * w_down.size,
            transcendentals=0,
        ),
    )
    split = 2 * slots * rows
    chip_sum = (keep[:split].astype(jnp.float32) + given.astype(jnp.float32)).astype(jnp.bfloat16)
    context, chip_sum = lax.optimization_barrier((left_context.transpose(1, 0, 2), chip_sum))
    arrived = [far(chip_sum[2 * rows * j : 2 * rows * (j + 1)], back, j) for j in range(slots)]
    rest, base = call(
        functools.partial(prepare_kernel, len(parts), rows),
        "prepare",
        [
            bf16((rows, features)),
            jax.ShapeDtypeStruct((rows, horizon, talker_width), jnp.float32),
        ],
        [table, context, frame_offset, conv_weight] + parts,
        scratch=[pltpu.VMEM((total, features), jnp.bfloat16)],
        megabytes=8,
        cost=pl.CostEstimate(
            flops=2 * rows * total * features, bytes_accessed=2 * total * features, transcendentals=0
        ),
    )
    arrived[0], rest, base = lax.optimization_barrier((arrived[0], rest, base))
    partial = keep[split:].astype(jnp.float32)
    for a in arrived:
        partial = partial + a.astype(jnp.float32)
    got = near(partial[rows:].astype(jnp.bfloat16))
    return call(
        owner_kernel,
        "owner",
        bf16((rows, horizon, talker_width)),
        [speech_count, partial, got, rest, talker_proj, base, conv_weight],
        scalars=1,
        megabytes=8,
    )


def local(thinker_rows, *rest):
    devices = lax.axis_size("ep")
    rows = thinker_rows.shape[0]
    small = rows <= CAP and rows == devices and devices % 4 == 0 and devices & (devices - 1) == 0
    return (local_gather if small else local_dispatch)(thinker_rows, *rest)


def solution(mesh):
    in_specs = (
        P(("groups", "ep"), None),
        P(("groups", "ep"), None),
        P(("groups", "ep"), None),
        P("ep", None, None),
        P("ep", None, None),
        P("ep", None, None),
        P(),
        P(("groups", "ep"), None),
        P(("groups", "ep")),
        P(("groups", "ep"), None, None),
        P(),
        P(),
    )
    out_specs = P(("groups", "ep"), None, None)
    return jax.shard_map(local, mesh=mesh, in_specs=in_specs, out_specs=out_specs, check_vma=False)
```

```python
import functools

import jax
import jax.numpy as jnp
import numpy as np
from jax import lax
from jax.experimental import pallas as pl
from jax.experimental.pallas import tpu as pltpu
from jax.sharding import PartitionSpec as P


CAP = 16
LANES = 128


def expert_block(block_rows, gate_mat, up_mat, down_mat):
    gate_act = jnp.dot(block_rows, gate_mat, preferred_element_type=jnp.float32)
    up_act = jnp.dot(block_rows, up_mat, preferred_element_type=jnp.float32)
    inner = (jax.nn.silu(gate_act) * up_act).astype(jnp.bfloat16)
    return jnp.dot(inner, down_mat, preferred_element_type=jnp.float32).astype(jnp.bfloat16)


def project(hidden, talker_proj):
    values = hidden.astype(jnp.float32)
    scaled = values * lax.rsqrt(jnp.mean(values * values, axis=-1, keepdims=True) + 1e-06)
    return jnp.dot(
        scaled.astype(jnp.bfloat16), talker_proj, preferred_element_type=jnp.float32
    ).astype(jnp.bfloat16)


def vocode(owned, speech_count, left_context, frame_offset, conv_weight):
    frames = owned.astype(jnp.float32)[:, None, :] + frame_offset[None, :, :]
    sequence = jnp.concatenate([left_context.astype(jnp.float32), frames], axis=1)
    taps = conv_weight.shape[0]
    horizon = frame_offset.shape[0]
    result = jnp.zeros_like(frames)
    for offset in range(taps):
        result = (
            result + conv_weight[offset][None, None, :] * sequence[:, offset : offset + horizon, :]
        )
    active = jnp.arange(horizon, dtype=jnp.int32)[None, :, None] < speech_count[:, None, None]
    return jnp.where(active, result, 0.0).astype(jnp.bfloat16)


def slot_positions(expert_ids, experts):
    flat_expert = expert_ids.reshape(-1)
    onehot = (flat_expert[:, None] == jnp.arange(experts, dtype=jnp.int32)[None, :]).astype(
        jnp.int32
    )
    position = jnp.sum((jnp.cumsum(onehot, axis=0) - onehot) * onehot, axis=1)
    return (flat_expert, position)


def run_and_return(buffer, w_gate, w_up, w_down):
    sources, slot_count, features = buffer.shape
    flattened = buffer.reshape(sources * slot_count, features)
    outputs = expert_block(flattened, w_gate[0], w_up[0], w_down[0]).reshape(
        sources, slot_count, features
    )
    return lax.all_to_all(outputs, "ep", split_axis=0, concat_axis=0, tiled=True)


def local_dispatch(
    thinker_rows,
    expert_ids,
    gate_weights,
    w_gate,
    w_up,
    w_down,
    talker_proj,
    talker_slot,
    speech_count,
    left_context,
    frame_offset,
    conv_weight,
):
    devices = lax.axis_size("ep")
    streams_here, features = thinker_rows.shape
    chosen = expert_ids.shape[1]
    flat_expert, position = slot_positions(expert_ids, devices)
    row_index = jnp.arange(streams_here * chosen, dtype=jnp.int32) // chosen
    outgoing = (
        jnp.zeros((devices, CAP, features), jnp.bfloat16)
        .at[flat_expert, position]
        .set(thinker_rows[row_index])
    )
    returned = run_and_return(
        lax.all_to_all(outgoing, "ep", split_axis=0, concat_axis=0, tiled=True),
        w_gate,
        w_up,
        w_down,
    )
    lookup = (
        returned[flat_expert, position].astype(jnp.float32).reshape(streams_here, chosen, features)
    )
    mixture = jnp.sum(gate_weights[:, :, None] * lookup, axis=1)
    hidden = (thinker_rows.astype(jnp.float32) + mixture).astype(jnp.bfloat16)
    slots = talker_slot[0]
    per_owner = streams_here // devices
    talker_rows = project(hidden, talker_proj)
    placed = (
        jnp.zeros_like(talker_rows)
        .at[slots]
        .set(talker_rows)
        .reshape(devices, per_owner, talker_rows.shape[1])
    )
    owned = lax.all_to_all(placed, "ep", split_axis=0, concat_axis=0, tiled=True).reshape(
        streams_here, talker_rows.shape[1]
    )
    return vocode(owned, speech_count, left_context, frame_offset, conv_weight)


def dot32(a, b):
    return jnp.dot(a, b, preferred_element_type=jnp.float32)


def sort_rows(experts, rows_ref, ids_ref, gates_ref, slot_ref, out_ref, at):
    rows, features = rows_ref.shape
    width = out_ref.shape[1] - features
    owner = lax.broadcasted_iota(jnp.int32, (rows, rows), 0)
    order = (owner == slot_ref[...]).astype(jnp.bfloat16)
    lane = lax.broadcasted_iota(jnp.int32, (width, rows), 0)
    expert = lane % experts
    gates = jnp.zeros((width, rows), jnp.float32)
    for j in range(ids_ref.shape[0]):
        gates = gates + jnp.where(expert == ids_ref[j : j + 1, :], gates_ref[j : j + 1, :], 0.0)
    high = gates.astype(jnp.bfloat16).astype(jnp.float32)
    middle = (gates - high).astype(jnp.bfloat16).astype(jnp.float32)
    low = gates - high - middle
    part = lane // experts
    packed = jnp.where(
        part == 0, high, jnp.where(part == 1, middle, jnp.where(part == 2, low, 0.0))
    ).astype(jnp.bfloat16)
    out_ref[at : at + rows, :features] = dot32(order, rows_ref[...]).astype(jnp.bfloat16)
    out_ref[at : at + rows, features:] = lax.dot_general(
        order, packed, (((1,), (1,)), ((), ())), preferred_element_type=jnp.float32
    ).astype(jnp.bfloat16)


def own_kernel(experts, rows_ref, ids_ref, gates_ref, slot_ref, out_ref):
    sort_rows(experts, rows_ref, ids_ref, gates_ref, slot_ref, out_ref, 0)


def pair_kernel(own_ref, other_ref, out_ref):
    rows = own_ref.shape[0]
    out_ref[:rows, :] = own_ref[...]
    out_ref[rows:, :] = other_ref[...]


def fetch_kernel(*refs):
    count = (len(refs) - 1) // 2
    sems = refs[-1]
    copies = [
        pltpu.make_async_copy(refs[i], refs[count + i], sems.at[i]) for i in range(count)
    ]
    for copy in copies:
        copy.start()
    for copy in copies:
        copy.wait()


def move_rows(me, rows, table_ref, target_ref):
    core = me % 2
    columns = table_ref.shape[1]
    origin = jnp.where(core == 0, table_ref[0:1, :], table_ref[1:2, :])
    owner = lax.broadcasted_iota(jnp.int32, (1, columns), 1) % rows
    target = jnp.where(core == 0, target_ref[:, 0:1], target_ref[:, 1:2])
    rank = lax.broadcasted_iota(jnp.int32, target.shape, 0) % rows
    hit = (origin == (target ^ rank)) & (owner == (target ^ me)) & (target >= 0)
    return jnp.where(hit, 1.0, 0.0).astype(jnp.bfloat16)


def activate(experts, parts, wg_ref, wu_ref, x_ref, inner_ref, first):
    me = lax.axis_index("ep")
    features, hidden = wg_ref.shape
    at = 0
    for part in parts:
        x_ref[at : at + part.shape[0], :] = part[...]
        at += part.shape[0]
    meta = x_ref[:, features:].astype(jnp.float32)
    lane = lax.broadcasted_iota(jnp.int32, (1, meta.shape[1]), 1)
    pick = (lane % experts == me) & (lane < 3 * experts)
    gate = jnp.sum(jnp.where(pick, meta, 0.0), axis=1, keepdims=True)
    step = min(256, hidden)
    for n in range(0, hidden, step):
        g = dot32(x_ref[:, :features], wg_ref[:, n : n + step])
        u = dot32(x_ref[:, :features], wu_ref[:, n : n + step])
        inner = (g * jax.nn.sigmoid(g) * u * gate).astype(jnp.bfloat16)
        inner_ref[first : first + at, n : n + step] = inner


def early_kernel(experts, wg_ref, wu_ref, *refs):
    activate(experts, refs[:-2], wg_ref, wu_ref, refs[-1], refs[-2], 0)


def late_kernel(experts, rows, table_ref, target_ref, wg_ref, wu_ref, wd_ref, early_ref, *refs):
    parts, (out_ref, inner_ref, x_ref) = refs[:-3], refs[-3:]
    first = early_ref.shape[0]
    inner_ref[:first, :] = early_ref[...]
    activate(experts, parts, wg_ref, wu_ref, x_ref, inner_ref, first)
    down_kernel(rows, table_ref, target_ref, wd_ref, inner_ref, out_ref)


def down_kernel(rows, table_ref, target_ref, wd_ref, inner_ref, *outs):
    me = lax.axis_index("ep")
    move = move_rows(me, rows, table_ref, target_ref)
    placed = dot32(move, inner_ref[...]).astype(jnp.bfloat16)
    features = wd_ref.shape[1]
    step = min(512, features)
    for n in range(0, features, step):
        y = dot32(placed, wd_ref[:, n : n + step]).astype(jnp.bfloat16)
        at = 0
        for out in outs:
            out[:, n : n + step] = y[at : at + out.shape[0]]
            at += out.shape[0]


def sum_kernel(ours_ref, given_ref, *outs):
    at = 0
    for out in outs:
        piece = slice(at, at + out.shape[0])
        total = ours_ref[piece, :].astype(jnp.float32) + given_ref[piece, :].astype(jnp.float32)
        out[...] = total.astype(jnp.bfloat16)
        at += out.shape[0]


def prepare_kernel(blocks, rows, table_ref, context_ref, offset_ref, conv_ref, *refs):
    parts, (rest_ref, base_ref, x_ref) = refs[:blocks], refs[blocks:]
    me = lax.axis_index("ep")
    features = rest_ref.shape[1]
    at = 0
    for part in parts:
        x_ref[at : at + part.shape[0], :] = part[:, :features]
        at += part.shape[0]
    columns = table_ref.shape[1]
    origin = jnp.where(me % 2 == 0, table_ref[0:1, :], table_ref[1:2, :])
    owner = lax.broadcasted_iota(jnp.int32, (1, columns), 1) % rows
    rank = lax.broadcasted_iota(jnp.int32, (rows, 1), 0)
    pick = jnp.where((origin == rank) & (owner == me), 1.0, 0.0).astype(jnp.bfloat16)
    rest_ref[...] = dot32(pick, x_ref[...]).astype(jnp.bfloat16)
    taps, horizon, past = conv_ref.shape[0], offset_ref.shape[0], context_ref.shape[0]
    context = [context_ref[i].astype(jnp.float32) for i in range(past)]
    for f in range(horizon):
        fixed = jnp.zeros((1, conv_ref.shape[1]), jnp.float32)
        for t in range(past - f, taps):
            i = f + t - past
            fixed = fixed + conv_ref[t : t + 1, :] * offset_ref[i : i + 1, :]
        total = jnp.broadcast_to(fixed, context[0].shape)
        for t in range(past - f):
            total = total + conv_ref[t : t + 1, :] * context[f + t]
        base_ref[:, f, :] = total


def owner_kernel(
    count_ref, mine_ref, got_ref, rest_ref, proj_ref, base_ref, conv_ref, out_ref
):
    me = lax.axis_index("ep")
    rows = rest_ref.shape[0]
    total = mine_ref[:rows, :] + got_ref[...].astype(jnp.float32)
    total = total + rest_ref[...].astype(jnp.float32)
    values = total.astype(jnp.bfloat16).astype(jnp.float32)
    normed = values * lax.rsqrt(jnp.mean(values * values, axis=-1, keepdims=True) + 1e-06)
    talker = dot32(normed.astype(jnp.bfloat16), proj_ref[...]).astype(jnp.bfloat16)
    one = lax.broadcasted_iota(jnp.int32, (rows, rows), 0)
    two = lax.broadcasted_iota(jnp.int32, (rows, rows), 1)
    order = jnp.where((one ^ two) == me, 1.0, 0.0).astype(jnp.bfloat16)
    owned = dot32(order, talker)
    taps, horizon = conv_ref.shape[0], base_ref.shape[1]
    frame = lax.broadcasted_iota(jnp.int32, (horizon, owned.shape[1]), 0)
    scale = jnp.zeros(frame.shape, jnp.float32)
    for t in range(taps):
        scale = scale + jnp.where(frame + t >= taps - 1, conv_ref[t : t + 1, :], 0.0)
    for q in range(rows):
        voice = base_ref[q] + scale * owned[q : q + 1, :]
        out_ref[q] = jnp.where(frame < count_ref[q], voice, 0.0).astype(jnp.bfloat16)


def vmem(count):
    return [pl.BlockSpec(memory_space=pltpu.VMEM)] * count


def gather_partners(chips):
    between = list(range(2, chips - 2))
    half = len(between) // 2
    return [
        [chips - 2, None] + between[:half],
        [chips - 1, 1] + between[half:],
    ]


def reduce_partners(chips):
    masks = list(range(chips - 1, 0, -1)) + [None]
    return [
        [m for k, m in enumerate(masks) if k % 4 in (0, 3)],
        [m for k, m in enumerate(masks) if k % 4 in (1, 2)],
    ]


def in_hbm(x):
    return pltpu.with_memory_space_constraint(x, pltpu.HBM)


def call(kernel, out_shape, operands, scalars=0, scratch=(), megabytes=4, cost=None, in_specs=None):
    several = isinstance(out_shape, (list, tuple))
    specs = [pl.BlockSpec(memory_space=pltpu.SMEM)] * scalars + vmem(len(operands) - scalars)
    return pl.pallas_call(
        kernel,
        out_shape=out_shape,
        in_specs=in_specs or specs,
        out_specs=vmem(len(out_shape)) if several else vmem(1)[0],
        scratch_shapes=list(scratch),
        compiler_params=pltpu.CompilerParams(vmem_limit_bytes=megabytes << 20),
        cost_estimate=cost,
    )(*operands)


def local_gather(
    thinker_rows,
    expert_ids,
    gate_weights,
    w_gate,
    w_up,
    w_down,
    talker_proj,
    talker_slot,
    speech_count,
    left_context,
    frame_offset,
    conv_weight,
):
    devices = lax.axis_size("ep")
    rows, features = thinker_rows.shape
    hidden = w_gate.shape[2]
    talker_width = talker_proj.shape[1]
    horizon = frame_offset.shape[0]
    lists = gather_partners(devices // 2)
    back = reduce_partners(devices // 2)
    slots = len(lists[0])
    width = -(-3 * devices // LANES) * LANES
    bf16 = functools.partial(jax.ShapeDtypeStruct, dtype=jnp.bfloat16)

    def far(x, chips, j):
        pairs = [(i, i ^ (chips[i % 2][j] * 2)) for i in range(devices) if chips[i % 2][j]]
        return lax.ppermute(x, "ep", pairs)

    def near(x, j=None):
        pairs = [(i, i ^ 1) for i in range(devices) if j is None or lists[i % 2][j]]
        return lax.ppermute(x, "ep", pairs)

    def side(chips, flip):
        blocks = [[-1, -1] if m is None else [2 * m + flip, 2 * m + 1 - flip] for m in chips]
        return [k for pair in blocks for k in pair]

    def spread(blocks):
        return np.repeat(np.array(blocks, np.int32), rows)

    first_slots, last_slots = range(slots // 2), range(slots // 2, slots)

    def arriving(c, chosen):
        some = [[chips[j] for j in chosen] for chips in (lists[c], lists[1 - c])]
        return side(some[0], 0) + side(some[1], 1)

    half = slots // 2
    table = np.stack(
        [spread([0, 1] + arriving(c, first_slots) + arriving(c, last_slots)) for c in range(2)]
    )
    keep_to = np.stack([spread(side(back[c], 0) + [0, 1]) for c in range(2)], axis=1)
    give_to = np.stack([spread(side(back[1 - c], 1)) for c in range(2)], axis=1)
    cut = 2 * rows * half
    rest_to = np.concatenate([give_to[cut:], keep_to])

    own = call(
        functools.partial(own_kernel, devices),
        bf16((rows, features + width)),
        [in_hbm(v) for v in (thinker_rows, expert_ids.T, gate_weights.T, talker_slot)],
        megabytes=4,
    )
    pair = call(pair_kernel, bf16((2 * rows, features + width)), [own, near(own)])
    pair, w_up, w_down = lax.optimization_barrier((pair, w_up, w_down))
    mine = [far(pair, lists, j) for j in range(slots)]
    w_up_here, w_down_here = call(
        fetch_kernel,
        [bf16(w_up.shape[1:]), bf16(w_down.shape[1:])],
        [in_hbm(w_up[0]), in_hbm(w_down[0])],
        in_specs=[pl.BlockSpec(memory_space=pltpu.HBM)] * 2,
        scratch=[pltpu.SemaphoreType.DMA((2,))],
        cost=pl.CostEstimate(flops=0, bytes_accessed=4 * w_up.size, transcendentals=0),
    )
    early_parts = [pair] + [mine[j] for j in first_slots] + [near(mine[j], j) for j in first_slots]
    early_rows = sum(p.shape[0] for p in early_parts)
    early = call(
        functools.partial(early_kernel, devices),
        bf16((early_rows, hidden)),
        [w_gate[0], w_up_here] + early_parts,
        scratch=[pltpu.VMEM((early_rows, features + width), jnp.bfloat16)],
        megabytes=10,
        cost=pl.CostEstimate(
            flops=4 * early_rows * features * hidden,
            bytes_accessed=4 * w_up.size,
            transcendentals=0,
        ),
    )
    late_parts = [mine[j] for j in last_slots]
    late_parts += [near(mine[j], j) for j in last_slots]
    late_rows = sum(p.shape[0] for p in late_parts)
    parts = early_parts + late_parts
    total = early_rows + late_rows
    give, inner = call(
        functools.partial(late_kernel, devices, rows),
        [bf16((cut, features)), bf16((total, hidden))],
        [table, give_to[:cut], w_gate[0], w_up_here, w_down_here, early] + late_parts,
        scratch=[pltpu.VMEM((late_rows, features + width), jnp.bfloat16)],
        megabytes=12,
    )
    given = [near(give)]
    give, *keep, here = call(
        functools.partial(down_kernel, rows),
        [bf16((cut, features))] * 3 + [bf16((2 * rows, features))],
        [table, rest_to, w_down_here, inner],
        megabytes=6,
        cost=pl.CostEstimate(
            flops=2 * rest_to.shape[0] * features * hidden,
            bytes_accessed=2 * w_down.size,
            transcendentals=0,
        ),
    )
    given.append(near(give))
    chip_sum = []
    for k in range(2):
        chip_sum += call(sum_kernel, [bf16((2 * rows, features))] * half, [keep[k], given[k]])
    arrived = [far(chip_sum[j], back, j) for j in range(slots)]
    context, _ = lax.optimization_barrier((left_context.transpose(1, 0, 2), chip_sum[-1]))
    rest, base = call(
        functools.partial(prepare_kernel, len(parts), rows),
        [
            bf16((rows, features)),
            jax.ShapeDtypeStruct((rows, horizon, talker_width), jnp.float32),
        ],
        [table, context, frame_offset, conv_weight] + parts,
        scratch=[pltpu.VMEM((total, features), jnp.bfloat16)],
        megabytes=8,
        cost=pl.CostEstimate(
            flops=2 * rows * total * features, bytes_accessed=2 * total * features, transcendentals=0
        ),
    )
    arrived[0], rest, base = lax.optimization_barrier((arrived[0], rest, base))
    partial = here.astype(jnp.float32)
    for a in arrived:
        partial = partial + a.astype(jnp.float32)
    got = near(partial[rows:].astype(jnp.bfloat16))
    return call(
        owner_kernel,
        bf16((rows, horizon, talker_width)),
        [speech_count, partial, got, rest, talker_proj, base, conv_weight],
        scalars=1,
        megabytes=8,
    )


def local(thinker_rows, *rest):
    devices = lax.axis_size("ep")
    rows = thinker_rows.shape[0]
    small = rows <= CAP and rows == devices and devices >= 8 and devices & (devices - 1) == 0
    if not small:
        return local_dispatch(thinker_rows, *rest)
    return local_gather(thinker_rows, *rest)


def solution(mesh):
    in_specs = (
        P(("groups", "ep"), None),
        P(("groups", "ep"), None),
        P(("groups", "ep"), None),
        P("ep", None, None),
        P("ep", None, None),
        P("ep", None, None),
        P(),
        P(("groups", "ep"), None),
        P(("groups", "ep")),
        P(("groups", "ep"), None, None),
        P(),
        P(),
    )
    out_specs = P(("groups", "ep"), None, None)
    return jax.shard_map(local, mesh=mesh, in_specs=in_specs, out_specs=out_specs, check_vma=False)
```

```python
import functools

import jax
import jax.numpy as jnp
import numpy as np
from jax import lax
from jax.experimental import pallas as pl
from jax.experimental.pallas import tpu as pltpu
from jax.sharding import PartitionSpec as P


CAP = 16
LANES = 128


def expert_block(block_rows, gate_mat, up_mat, down_mat):
    gate_act = jnp.dot(block_rows, gate_mat, preferred_element_type=jnp.float32)
    up_act = jnp.dot(block_rows, up_mat, preferred_element_type=jnp.float32)
    inner = (jax.nn.silu(gate_act) * up_act).astype(jnp.bfloat16)
    return jnp.dot(inner, down_mat, preferred_element_type=jnp.float32).astype(jnp.bfloat16)


def project(hidden, talker_proj):
    values = hidden.astype(jnp.float32)
    scaled = values * lax.rsqrt(jnp.mean(values * values, axis=-1, keepdims=True) + 1e-06)
    return jnp.dot(
        scaled.astype(jnp.bfloat16), talker_proj, preferred_element_type=jnp.float32
    ).astype(jnp.bfloat16)


def vocode(owned, speech_count, left_context, frame_offset, conv_weight):
    frames = owned.astype(jnp.float32)[:, None, :] + frame_offset[None, :, :]
    sequence = jnp.concatenate([left_context.astype(jnp.float32), frames], axis=1)
    taps = conv_weight.shape[0]
    horizon = frame_offset.shape[0]
    result = jnp.zeros_like(frames)
    for offset in range(taps):
        result = (
            result + conv_weight[offset][None, None, :] * sequence[:, offset : offset + horizon, :]
        )
    active = jnp.arange(horizon, dtype=jnp.int32)[None, :, None] < speech_count[:, None, None]
    return jnp.where(active, result, 0.0).astype(jnp.bfloat16)


def slot_positions(expert_ids, experts):
    flat_expert = expert_ids.reshape(-1)
    onehot = (flat_expert[:, None] == jnp.arange(experts, dtype=jnp.int32)[None, :]).astype(
        jnp.int32
    )
    position = jnp.sum((jnp.cumsum(onehot, axis=0) - onehot) * onehot, axis=1)
    return (flat_expert, position)


def run_and_return(buffer, w_gate, w_up, w_down):
    sources, slot_count, features = buffer.shape
    flattened = buffer.reshape(sources * slot_count, features)
    outputs = expert_block(flattened, w_gate[0], w_up[0], w_down[0]).reshape(
        sources, slot_count, features
    )
    return lax.all_to_all(outputs, "ep", split_axis=0, concat_axis=0, tiled=True)


def local_dispatch(
    thinker_rows,
    expert_ids,
    gate_weights,
    w_gate,
    w_up,
    w_down,
    talker_proj,
    talker_slot,
    speech_count,
    left_context,
    frame_offset,
    conv_weight,
):
    devices = lax.axis_size("ep")
    streams_here, features = thinker_rows.shape
    chosen = expert_ids.shape[1]
    flat_expert, position = slot_positions(expert_ids, devices)
    row_index = jnp.arange(streams_here * chosen, dtype=jnp.int32) // chosen
    outgoing = (
        jnp.zeros((devices, CAP, features), jnp.bfloat16)
        .at[flat_expert, position]
        .set(thinker_rows[row_index])
    )
    returned = run_and_return(
        lax.all_to_all(outgoing, "ep", split_axis=0, concat_axis=0, tiled=True),
        w_gate,
        w_up,
        w_down,
    )
    lookup = (
        returned[flat_expert, position].astype(jnp.float32).reshape(streams_here, chosen, features)
    )
    mixture = jnp.sum(gate_weights[:, :, None] * lookup, axis=1)
    hidden = (thinker_rows.astype(jnp.float32) + mixture).astype(jnp.bfloat16)
    slots = talker_slot[0]
    per_owner = streams_here // devices
    talker_rows = project(hidden, talker_proj)
    placed = (
        jnp.zeros_like(talker_rows)
        .at[slots]
        .set(talker_rows)
        .reshape(devices, per_owner, talker_rows.shape[1])
    )
    owned = lax.all_to_all(placed, "ep", split_axis=0, concat_axis=0, tiled=True).reshape(
        streams_here, talker_rows.shape[1]
    )
    return vocode(owned, speech_count, left_context, frame_offset, conv_weight)


def dot32(a, b):
    return jnp.dot(a, b, preferred_element_type=jnp.float32)


def sort_rows(experts, rows_ref, ids_ref, gates_ref, slot_ref, out_ref, at):
    rows, features = rows_ref.shape
    width = out_ref.shape[1] - features
    owner = lax.broadcasted_iota(jnp.int32, (rows, rows), 0)
    order = (owner == slot_ref[...]).astype(jnp.bfloat16)
    lane = lax.broadcasted_iota(jnp.int32, (width, rows), 0)
    expert = lane % experts
    gates = jnp.zeros((width, rows), jnp.float32)
    for j in range(ids_ref.shape[0]):
        gates = gates + jnp.where(expert == ids_ref[j : j + 1, :], gates_ref[j : j + 1, :], 0.0)
    high = gates.astype(jnp.bfloat16).astype(jnp.float32)
    middle = (gates - high).astype(jnp.bfloat16).astype(jnp.float32)
    low = gates - high - middle
    part = lane // experts
    packed = jnp.where(
        part == 0, high, jnp.where(part == 1, middle, jnp.where(part == 2, low, 0.0))
    ).astype(jnp.bfloat16)
    out_ref[at : at + rows, :features] = dot32(order, rows_ref[...]).astype(jnp.bfloat16)
    out_ref[at : at + rows, features:] = lax.dot_general(
        order, packed, (((1,), (1,)), ((), ())), preferred_element_type=jnp.float32
    ).astype(jnp.bfloat16)


def own_kernel(experts, rows_ref, ids_ref, gates_ref, slot_ref, out_ref):
    sort_rows(experts, rows_ref, ids_ref, gates_ref, slot_ref, out_ref, 0)


def pair_kernel(own_ref, other_ref, out_ref):
    rows = own_ref.shape[0]
    out_ref[:rows, :] = own_ref[...]
    out_ref[rows:, :] = other_ref[...]


def fetch_kernel(*refs):
    count = (len(refs) - 1) // 2
    sems = refs[-1]
    copies = [
        pltpu.make_async_copy(refs[i], refs[count + i], sems.at[i]) for i in range(count)
    ]
    for copy in copies:
        copy.start()
    for copy in copies:
        copy.wait()


def move_rows(me, rows, table_ref, target_ref):
    core = me % 2
    columns = table_ref.shape[1]
    origin = jnp.where(core == 0, table_ref[0:1, :], table_ref[1:2, :])
    owner = lax.broadcasted_iota(jnp.int32, (1, columns), 1) % rows
    target = jnp.where(core == 0, target_ref[:, 0:1], target_ref[:, 1:2])
    rank = lax.broadcasted_iota(jnp.int32, target.shape, 0) % rows
    hit = (origin == (target ^ rank)) & (owner == (target ^ me)) & (target >= 0)
    return jnp.where(hit, 1.0, 0.0).astype(jnp.bfloat16)


def activate(experts, parts, wg_ref, wu_ref, x_ref, inner_ref, first):
    me = lax.axis_index("ep")
    features, hidden = wg_ref.shape
    at = 0
    for part in parts:
        x_ref[at : at + part.shape[0], :] = part[...]
        at += part.shape[0]
    meta = x_ref[:, features:].astype(jnp.float32)
    lane = lax.broadcasted_iota(jnp.int32, (1, meta.shape[1]), 1)
    pick = (lane % experts == me) & (lane < 3 * experts)
    gate = jnp.sum(jnp.where(pick, meta, 0.0), axis=1, keepdims=True)
    step = min(256, hidden)
    for n in range(0, hidden, step):
        g = dot32(x_ref[:, :features], wg_ref[:, n : n + step])
        u = dot32(x_ref[:, :features], wu_ref[:, n : n + step])
        inner = (g * jax.nn.sigmoid(g) * u * gate).astype(jnp.bfloat16)
        inner_ref[first : first + at, n : n + step] = inner


def early_kernel(experts, wg_ref, wu_ref, *refs):
    activate(experts, refs[:-2], wg_ref, wu_ref, refs[-1], refs[-2], 0)


def late_kernel(experts, rows, table_ref, target_ref, wg_ref, wu_ref, wd_ref, early_ref, *refs):
    parts, (out_ref, placed_ref, inner_ref, x_ref) = refs[:-4], refs[-4:]
    first = early_ref.shape[0]
    inner_ref[:first, :] = early_ref[...]
    activate(experts, parts, wg_ref, wu_ref, x_ref, inner_ref, first)
    move = move_rows(lax.axis_index("ep"), rows, table_ref, target_ref)
    placed = dot32(move, inner_ref[...]).astype(jnp.bfloat16)
    cut = out_ref.shape[0]
    placed_ref[...] = placed[cut:]
    down(placed[:cut], wd_ref, [out_ref])


def down(placed, wd_ref, outs):
    features = wd_ref.shape[1]
    step = min(512, features)
    for n in range(0, features, step):
        y = dot32(placed, wd_ref[:, n : n + step]).astype(jnp.bfloat16)
        at = 0
        for out in outs:
            out[:, n : n + step] = y[at : at + out.shape[0]]
            at += out.shape[0]


def rest_kernel(placed_ref, wd_ref, *outs):
    down(placed_ref[...], wd_ref, outs)


def sum_kernel(ours_ref, given_ref, *outs):
    at = 0
    for out in outs:
        piece = slice(at, at + out.shape[0])
        total = ours_ref[piece, :].astype(jnp.float32) + given_ref[piece, :].astype(jnp.float32)
        out[...] = total.astype(jnp.bfloat16)
        at += out.shape[0]


def prepare_kernel(
    blocks, rows, count_ref, table_ref, context_ref, offset_ref, conv_ref, *refs
):
    parts, (rest_ref, base_ref, scale_ref, x_ref) = refs[:blocks], refs[blocks:]
    me = lax.axis_index("ep")
    features = rest_ref.shape[1]
    at = 0
    for part in parts:
        x_ref[at : at + part.shape[0], :] = part[:, :features]
        at += part.shape[0]
    columns = table_ref.shape[1]
    origin = jnp.where(me % 2 == 0, table_ref[0:1, :], table_ref[1:2, :])
    owner = lax.broadcasted_iota(jnp.int32, (1, columns), 1) % rows
    rank = lax.broadcasted_iota(jnp.int32, (rows, 1), 0)
    pick = jnp.where((origin == rank) & (owner == me), 1.0, 0.0).astype(jnp.bfloat16)
    rest_ref[...] = dot32(pick, x_ref[...]).astype(jnp.bfloat16)
    taps, horizon, past = conv_ref.shape[0], offset_ref.shape[0], context_ref.shape[0]
    context = [context_ref[i].astype(jnp.float32) for i in range(past)]
    stream = lax.broadcasted_iota(jnp.int32, (rows, 1), 0)
    count = jnp.zeros((rows, 1), jnp.int32)
    for q in range(rows):
        count = jnp.where(stream == q, count_ref[q], count)
    for f in range(horizon):
        fixed = jnp.zeros((1, conv_ref.shape[1]), jnp.float32)
        scale = jnp.zeros((1, conv_ref.shape[1]), jnp.float32)
        for t in range(past - f, taps):
            i = f + t - past
            fixed = fixed + conv_ref[t : t + 1, :] * offset_ref[i : i + 1, :]
            scale = scale + conv_ref[t : t + 1, :]
        total = jnp.broadcast_to(fixed, context[0].shape)
        for t in range(past - f):
            total = total + conv_ref[t : t + 1, :] * context[f + t]
        base_ref[:, f, :] = jnp.where(f < count, total, 0.0)
        scale_ref[:, f, :] = jnp.where(f < count, jnp.broadcast_to(scale, total.shape), 0.0)


def owner_kernel(mine_ref, got_ref, rest_ref, proj_ref, base_ref, scale_ref, out_ref):
    me = lax.axis_index("ep")
    rows = rest_ref.shape[0]
    total = mine_ref[:rows, :] + got_ref[...].astype(jnp.float32)
    total = total + rest_ref[...].astype(jnp.float32)
    values = total.astype(jnp.bfloat16).astype(jnp.float32)
    normed = values * lax.rsqrt(jnp.mean(values * values, axis=-1, keepdims=True) + 1e-06)
    talker = dot32(normed.astype(jnp.bfloat16), proj_ref[...]).astype(jnp.bfloat16)
    one = lax.broadcasted_iota(jnp.int32, (rows, rows), 0)
    two = lax.broadcasted_iota(jnp.int32, (rows, rows), 1)
    order = jnp.where((one ^ two) == me, 1.0, 0.0).astype(jnp.bfloat16)
    owned = dot32(order, talker)
    for q in range(rows):
        voice = base_ref[q] + scale_ref[q] * owned[q : q + 1, :]
        out_ref[q] = voice.astype(jnp.bfloat16)


def vmem(count):
    return [pl.BlockSpec(memory_space=pltpu.VMEM)] * count


def gather_partners(chips):
    between = list(range(2, chips - 2))
    half = len(between) // 2
    return [
        [chips - 2, None] + between[:half],
        [chips - 1, 1] + between[half:],
    ]


def reduce_partners(chips):
    masks = list(range(chips - 1, 0, -1)) + [None]
    return [
        [m for k, m in enumerate(masks) if k % 4 in (0, 3)],
        [m for k, m in enumerate(masks) if k % 4 in (1, 2)],
    ]


def in_hbm(x):
    return pltpu.with_memory_space_constraint(x, pltpu.HBM)


def call(kernel, out_shape, operands, scalars=0, scratch=(), megabytes=4, cost=None, in_specs=None):
    several = isinstance(out_shape, (list, tuple))
    specs = [pl.BlockSpec(memory_space=pltpu.SMEM)] * scalars + vmem(len(operands) - scalars)
    return pl.pallas_call(
        kernel,
        out_shape=out_shape,
        in_specs=in_specs or specs,
        out_specs=vmem(len(out_shape)) if several else vmem(1)[0],
        scratch_shapes=list(scratch),
        compiler_params=pltpu.CompilerParams(vmem_limit_bytes=megabytes << 20),
        cost_estimate=cost,
    )(*operands)


def local_gather(
    thinker_rows,
    expert_ids,
    gate_weights,
    w_gate,
    w_up,
    w_down,
    talker_proj,
    talker_slot,
    speech_count,
    left_context,
    frame_offset,
    conv_weight,
):
    devices = lax.axis_size("ep")
    rows, features = thinker_rows.shape
    hidden = w_gate.shape[2]
    talker_width = talker_proj.shape[1]
    horizon = frame_offset.shape[0]
    lists = gather_partners(devices // 2)
    back = reduce_partners(devices // 2)
    slots = len(lists[0])
    width = -(-3 * devices // LANES) * LANES
    bf16 = functools.partial(jax.ShapeDtypeStruct, dtype=jnp.bfloat16)

    def far(x, chips, j):
        pairs = [(i, i ^ (chips[i % 2][j] * 2)) for i in range(devices) if chips[i % 2][j]]
        return lax.ppermute(x, "ep", pairs)

    def near(x, j=None):
        pairs = [(i, i ^ 1) for i in range(devices) if j is None or lists[i % 2][j]]
        return lax.ppermute(x, "ep", pairs)

    def side(chips, flip):
        blocks = [[-1, -1] if m is None else [2 * m + flip, 2 * m + 1 - flip] for m in chips]
        return [k for pair in blocks for k in pair]

    def spread(blocks):
        return np.repeat(np.array(blocks, np.int32), rows)

    first_slots, last_slots = range(slots // 2), range(slots // 2, slots)

    def arriving(c, chosen):
        some = [[chips[j] for j in chosen] for chips in (lists[c], lists[1 - c])]
        return side(some[0], 0) + side(some[1], 1)

    half = slots // 2
    table = np.stack(
        [spread([0, 1] + arriving(c, first_slots) + arriving(c, last_slots)) for c in range(2)]
    )
    keep_to = np.stack([spread(side(back[c], 0) + [0, 1]) for c in range(2)], axis=1)
    give_to = np.stack([spread(side(back[1 - c], 1)) for c in range(2)], axis=1)
    cut = 2 * rows * half
    target = np.concatenate([give_to, keep_to])

    own = call(
        functools.partial(own_kernel, devices),
        bf16((rows, features + width)),
        [in_hbm(v) for v in (thinker_rows, expert_ids.T, gate_weights.T, talker_slot)],
        megabytes=4,
    )
    pair = call(pair_kernel, bf16((2 * rows, features + width)), [own, near(own)])
    pair, w_up, w_down = lax.optimization_barrier((pair, w_up, w_down))
    mine = [far(pair, lists, j) for j in range(slots)]
    w_up_here, w_down_here = call(
        fetch_kernel,
        [bf16(w_up.shape[1:]), bf16(w_down.shape[1:])],
        [in_hbm(w_up[0]), in_hbm(w_down[0])],
        in_specs=[pl.BlockSpec(memory_space=pltpu.HBM)] * 2,
        scratch=[pltpu.SemaphoreType.DMA((2,))],
        cost=pl.CostEstimate(flops=0, bytes_accessed=4 * w_up.size, transcendentals=0),
    )
    early_parts = [pair] + [mine[j] for j in first_slots] + [near(mine[j], j) for j in first_slots]
    early_rows = sum(p.shape[0] for p in early_parts)
    early = call(
        functools.partial(early_kernel, devices),
        bf16((early_rows, hidden)),
        [w_gate[0], w_up_here] + early_parts,
        scratch=[pltpu.VMEM((early_rows, features + width), jnp.bfloat16)],
        megabytes=10,
        cost=pl.CostEstimate(
            flops=4 * early_rows * features * hidden,
            bytes_accessed=4 * w_up.size,
            transcendentals=0,
        ),
    )
    late_parts = [mine[j] for j in last_slots]
    late_parts += [near(mine[j], j) for j in last_slots]
    late_rows = sum(p.shape[0] for p in late_parts)
    parts = early_parts + late_parts
    total = early_rows + late_rows
    give, placed = call(
        functools.partial(late_kernel, devices, rows),
        [bf16((cut, features)), bf16((target.shape[0] - cut, hidden))],
        [table, target, w_gate[0], w_up_here, w_down_here, early] + late_parts,
        scratch=[
            pltpu.VMEM((total, hidden), jnp.bfloat16),
            pltpu.VMEM((late_rows, features + width), jnp.bfloat16),
        ],
        megabytes=12,
    )
    given = [near(give)]
    give, *keep, here = call(
        rest_kernel,
        [bf16((cut, features))] * 3 + [bf16((2 * rows, features))],
        [placed, w_down_here],
        megabytes=6,
        cost=pl.CostEstimate(
            flops=2 * target.shape[0] * features * hidden,
            bytes_accessed=2 * w_down.size,
            transcendentals=0,
        ),
    )
    given.append(near(give))
    chip_sum = []
    for k in range(2):
        chip_sum += call(sum_kernel, [bf16((2 * rows, features))] * half, [keep[k], given[k]])
    arrived = [far(chip_sum[j], back, j) for j in range(slots)]
    context, _ = lax.optimization_barrier((left_context.transpose(1, 0, 2), chip_sum[-1]))
    frames = jax.ShapeDtypeStruct((rows, horizon, talker_width), jnp.float32)
    rest, base, scale = call(
        functools.partial(prepare_kernel, len(parts), rows),
        [bf16((rows, features)), frames, frames],
        [speech_count, table, context, frame_offset, conv_weight] + parts,
        scalars=1,
        scratch=[pltpu.VMEM((total, features), jnp.bfloat16)],
        megabytes=8,
        cost=pl.CostEstimate(
            flops=2 * rows * total * features, bytes_accessed=2 * total * features, transcendentals=0
        ),
    )
    arrived[0], rest, base, scale = lax.optimization_barrier((arrived[0], rest, base, scale))
    partial = here.astype(jnp.float32)
    for a in arrived:
        partial = partial + a.astype(jnp.float32)
    got = near(partial[rows:].astype(jnp.bfloat16))
    return call(
        owner_kernel,
        bf16((rows, horizon, talker_width)),
        [partial, got, rest, talker_proj, base, scale],
        megabytes=8,
    )


def local(thinker_rows, *rest):
    devices = lax.axis_size("ep")
    rows = thinker_rows.shape[0]
    small = rows <= CAP and rows == devices and devices >= 8 and devices & (devices - 1) == 0
    if not small:
        return local_dispatch(thinker_rows, *rest)
    return local_gather(thinker_rows, *rest)


def solution(mesh):
    in_specs = (
        P(("groups", "ep"), None),
        P(("groups", "ep"), None),
        P(("groups", "ep"), None),
        P("ep", None, None),
        P("ep", None, None),
        P("ep", None, None),
        P(),
        P(("groups", "ep"), None),
        P(("groups", "ep")),
        P(("groups", "ep"), None, None),
        P(),
        P(),
    )
    out_specs = P(("groups", "ep"), None, None)
    return jax.shard_map(local, mesh=mesh, in_specs=in_specs, out_specs=out_specs, check_vma=False)
```

```python
import functools

import jax
import jax.numpy as jnp
import numpy as np
from jax import lax
from jax.experimental import pallas as pl
from jax.experimental.pallas import tpu as pltpu
from jax.sharding import PartitionSpec as P


CAP = 16
LANES = 128


def expert_block(block_rows, gate_mat, up_mat, down_mat):
    gate_act = jnp.dot(block_rows, gate_mat, preferred_element_type=jnp.float32)
    up_act = jnp.dot(block_rows, up_mat, preferred_element_type=jnp.float32)
    inner = (jax.nn.silu(gate_act) * up_act).astype(jnp.bfloat16)
    return jnp.dot(inner, down_mat, preferred_element_type=jnp.float32).astype(jnp.bfloat16)


def project(hidden, talker_proj):
    values = hidden.astype(jnp.float32)
    scaled = values * lax.rsqrt(jnp.mean(values * values, axis=-1, keepdims=True) + 1e-06)
    return jnp.dot(
        scaled.astype(jnp.bfloat16), talker_proj, preferred_element_type=jnp.float32
    ).astype(jnp.bfloat16)


def vocode(owned, speech_count, left_context, frame_offset, conv_weight):
    frames = owned.astype(jnp.float32)[:, None, :] + frame_offset[None, :, :]
    sequence = jnp.concatenate([left_context.astype(jnp.float32), frames], axis=1)
    taps = conv_weight.shape[0]
    horizon = frame_offset.shape[0]
    result = jnp.zeros_like(frames)
    for offset in range(taps):
        result = (
            result + conv_weight[offset][None, None, :] * sequence[:, offset : offset + horizon, :]
        )
    active = jnp.arange(horizon, dtype=jnp.int32)[None, :, None] < speech_count[:, None, None]
    return jnp.where(active, result, 0.0).astype(jnp.bfloat16)


def slot_positions(expert_ids, experts):
    flat_expert = expert_ids.reshape(-1)
    onehot = (flat_expert[:, None] == jnp.arange(experts, dtype=jnp.int32)[None, :]).astype(
        jnp.int32
    )
    position = jnp.sum((jnp.cumsum(onehot, axis=0) - onehot) * onehot, axis=1)
    return (flat_expert, position)


def run_and_return(buffer, w_gate, w_up, w_down):
    sources, slot_count, features = buffer.shape
    flattened = buffer.reshape(sources * slot_count, features)
    outputs = expert_block(flattened, w_gate[0], w_up[0], w_down[0]).reshape(
        sources, slot_count, features
    )
    return lax.all_to_all(outputs, "ep", split_axis=0, concat_axis=0, tiled=True)


def local_dispatch(
    thinker_rows,
    expert_ids,
    gate_weights,
    w_gate,
    w_up,
    w_down,
    talker_proj,
    talker_slot,
    speech_count,
    left_context,
    frame_offset,
    conv_weight,
):
    devices = lax.axis_size("ep")
    streams_here, features = thinker_rows.shape
    chosen = expert_ids.shape[1]
    flat_expert, position = slot_positions(expert_ids, devices)
    row_index = jnp.arange(streams_here * chosen, dtype=jnp.int32) // chosen
    outgoing = (
        jnp.zeros((devices, CAP, features), jnp.bfloat16)
        .at[flat_expert, position]
        .set(thinker_rows[row_index])
    )
    returned = run_and_return(
        lax.all_to_all(outgoing, "ep", split_axis=0, concat_axis=0, tiled=True),
        w_gate,
        w_up,
        w_down,
    )
    lookup = (
        returned[flat_expert, position].astype(jnp.float32).reshape(streams_here, chosen, features)
    )
    mixture = jnp.sum(gate_weights[:, :, None] * lookup, axis=1)
    hidden = (thinker_rows.astype(jnp.float32) + mixture).astype(jnp.bfloat16)
    slots = talker_slot[0]
    per_owner = streams_here // devices
    talker_rows = project(hidden, talker_proj)
    placed = (
        jnp.zeros_like(talker_rows)
        .at[slots]
        .set(talker_rows)
        .reshape(devices, per_owner, talker_rows.shape[1])
    )
    owned = lax.all_to_all(placed, "ep", split_axis=0, concat_axis=0, tiled=True).reshape(
        streams_here, talker_rows.shape[1]
    )
    return vocode(owned, speech_count, left_context, frame_offset, conv_weight)


def dot32(a, b):
    return jnp.dot(a, b, preferred_element_type=jnp.float32)


def sort_rows(experts, rows_ref, ids_ref, gates_ref, slot_ref, out_ref, at):
    rows, features = rows_ref.shape
    width = out_ref.shape[1] - features
    owner = lax.broadcasted_iota(jnp.int32, (rows, rows), 0)
    order = (owner == slot_ref[...]).astype(jnp.bfloat16)
    lane = lax.broadcasted_iota(jnp.int32, (width, rows), 0)
    expert = lane % experts
    gates = jnp.zeros((width, rows), jnp.float32)
    for j in range(ids_ref.shape[0]):
        gates = gates + jnp.where(expert == ids_ref[j : j + 1, :], gates_ref[j : j + 1, :], 0.0)
    high = gates.astype(jnp.bfloat16).astype(jnp.float32)
    middle = (gates - high).astype(jnp.bfloat16).astype(jnp.float32)
    low = gates - high - middle
    part = lane // experts
    packed = jnp.where(
        part == 0, high, jnp.where(part == 1, middle, jnp.where(part == 2, low, 0.0))
    ).astype(jnp.bfloat16)
    out_ref[at : at + rows, :features] = dot32(order, rows_ref[...]).astype(jnp.bfloat16)
    out_ref[at : at + rows, features:] = lax.dot_general(
        order, packed, (((1,), (1,)), ((), ())), preferred_element_type=jnp.float32
    ).astype(jnp.bfloat16)


def own_kernel(experts, rows_ref, ids_ref, gates_ref, slot_ref, out_ref):
    sort_rows(experts, rows_ref, ids_ref, gates_ref, slot_ref, out_ref, 0)


def pair_kernel(own_ref, other_ref, out_ref):
    rows = own_ref.shape[0]
    out_ref[:rows, :] = own_ref[...]
    out_ref[rows:, :] = other_ref[...]


def fetch_kernel(*refs):
    count = (len(refs) - 1) // 2
    sems = refs[-1]
    copies = [
        pltpu.make_async_copy(refs[i], refs[count + i], sems.at[i]) for i in range(count)
    ]
    for copy in copies:
        copy.start()
    for copy in copies:
        copy.wait()


def move_rows(me, rows, table_ref, target_ref):
    core = me % 2
    columns = table_ref.shape[1]
    origin = jnp.where(core == 0, table_ref[0:1, :], table_ref[1:2, :])
    owner = lax.broadcasted_iota(jnp.int32, (1, columns), 1) % rows
    target = jnp.where(core == 0, target_ref[:, 0:1], target_ref[:, 1:2])
    rank = lax.broadcasted_iota(jnp.int32, target.shape, 0) % rows
    hit = (origin == (target ^ rank)) & (owner == (target ^ me)) & (target >= 0)
    return jnp.where(hit, 1.0, 0.0).astype(jnp.bfloat16)


def activate(experts, parts, wg_ref, wu_ref, x_ref, inner_ref, first):
    me = lax.axis_index("ep")
    features, hidden = wg_ref.shape
    at = 0
    for part in parts:
        x_ref[at : at + part.shape[0], :] = part[...]
        at += part.shape[0]
    meta = x_ref[:, features:].astype(jnp.float32)
    lane = lax.broadcasted_iota(jnp.int32, (1, meta.shape[1]), 1)
    pick = (lane % experts == me) & (lane < 3 * experts)
    gate = jnp.sum(jnp.where(pick, meta, 0.0), axis=1, keepdims=True)
    step = min(256, hidden)
    for n in range(0, hidden, step):
        g = dot32(x_ref[:, :features], wg_ref[:, n : n + step])
        u = dot32(x_ref[:, :features], wu_ref[:, n : n + step])
        inner = (g * jax.nn.sigmoid(g) * u * gate).astype(jnp.bfloat16)
        inner_ref[first : first + at, n : n + step] = inner


def early_kernel(experts, wg_ref, wu_ref, *refs):
    activate(experts, refs[:-2], wg_ref, wu_ref, refs[-1], refs[-2], 0)


def late_kernel(experts, rows, table_ref, target_ref, wg_ref, wu_ref, wd_ref, early_ref, *refs):
    parts, (out_ref, placed_ref, inner_ref, x_ref) = refs[:-4], refs[-4:]
    first = early_ref.shape[0]
    inner_ref[:first, :] = early_ref[...]
    activate(experts, parts, wg_ref, wu_ref, x_ref, inner_ref, first)
    move = move_rows(lax.axis_index("ep"), rows, table_ref, target_ref)
    placed = dot32(move, inner_ref[...]).astype(jnp.bfloat16)
    cut = out_ref.shape[0]
    placed_ref[...] = placed[cut:]
    down(placed[:cut], wd_ref, [out_ref])


def down(placed, wd_ref, outs):
    features = wd_ref.shape[1]
    step = min(512, features)
    for n in range(0, features, step):
        y = dot32(placed, wd_ref[:, n : n + step]).astype(jnp.bfloat16)
        at = 0
        for out in outs:
            out[:, n : n + step] = y[at : at + out.shape[0]]
            at += out.shape[0]


def rest_kernel(placed_ref, wd_ref, *outs):
    down(placed_ref[...], wd_ref, outs)


def sum_kernel(ours_ref, given_ref, *outs):
    at = 0
    for out in outs:
        piece = slice(at, at + out.shape[0])
        total = ours_ref[piece, :].astype(jnp.float32) + given_ref[piece, :].astype(jnp.float32)
        out[...] = total.astype(jnp.bfloat16)
        at += out.shape[0]


def prepare_kernel(
    blocks, rows, count_ref, table_ref, context_ref, offset_ref, conv_ref, *refs
):
    parts, (rest_ref, base_ref, scale_ref, x_ref) = refs[:blocks], refs[blocks:]
    me = lax.axis_index("ep")
    features = rest_ref.shape[1]
    at = 0
    for part in parts:
        x_ref[at : at + part.shape[0], :] = part[:, :features]
        at += part.shape[0]
    columns = table_ref.shape[1]
    origin = jnp.where(me % 2 == 0, table_ref[0:1, :], table_ref[1:2, :])
    owner = lax.broadcasted_iota(jnp.int32, (1, columns), 1) % rows
    rank = lax.broadcasted_iota(jnp.int32, (rows, 1), 0)
    pick = jnp.where((origin == rank) & (owner == me), 1.0, 0.0).astype(jnp.bfloat16)
    rest_ref[...] = dot32(pick, x_ref[...]).astype(jnp.bfloat16)
    taps, horizon, past = conv_ref.shape[0], offset_ref.shape[0], context_ref.shape[0]
    context = [context_ref[i].astype(jnp.float32) for i in range(past)]
    stream = lax.broadcasted_iota(jnp.int32, (rows, 1), 0)
    count = jnp.zeros((rows, 1), jnp.int32)
    for q in range(rows):
        count = jnp.where(stream == q, count_ref[q], count)
    for f in range(horizon):
        fixed = jnp.zeros((1, conv_ref.shape[1]), jnp.float32)
        scale = jnp.zeros((1, conv_ref.shape[1]), jnp.float32)
        for t in range(past - f, taps):
            i = f + t - past
            fixed = fixed + conv_ref[t : t + 1, :] * offset_ref[i : i + 1, :]
            scale = scale + conv_ref[t : t + 1, :]
        total = jnp.broadcast_to(fixed, context[0].shape)
        for t in range(past - f):
            total = total + conv_ref[t : t + 1, :] * context[f + t]
        base_ref[:, f, :] = jnp.where(f < count, total, 0.0)
        scale_ref[:, f, :] = jnp.where(f < count, jnp.broadcast_to(scale, total.shape), 0.0)


def owner_kernel(mine_ref, got_ref, rest_ref, proj_ref, base_ref, scale_ref, out_ref):
    me = lax.axis_index("ep")
    rows = rest_ref.shape[0]
    total = mine_ref[:rows, :] + got_ref[...].astype(jnp.float32)
    total = total + rest_ref[...].astype(jnp.float32)
    values = total.astype(jnp.bfloat16).astype(jnp.float32)
    normed = values * lax.rsqrt(jnp.mean(values * values, axis=-1, keepdims=True) + 1e-06)
    talker = dot32(normed.astype(jnp.bfloat16), proj_ref[...]).astype(jnp.bfloat16)
    one = lax.broadcasted_iota(jnp.int32, (rows, rows), 0)
    two = lax.broadcasted_iota(jnp.int32, (rows, rows), 1)
    order = jnp.where((one ^ two) == me, 1.0, 0.0).astype(jnp.bfloat16)
    owned = dot32(order, talker)
    for q in range(rows):
        voice = base_ref[q] + scale_ref[q] * owned[q : q + 1, :]
        out_ref[q] = voice.astype(jnp.bfloat16)


def vmem(count):
    return [pl.BlockSpec(memory_space=pltpu.VMEM)] * count


def gather_partners(chips, across):
    others = [m for m in range(1, chips) if m != across]
    return [others[-2:-1] + others[:-2][0::2], others[-1:] + others[:-2][1::2]]


def reduce_partners(chips):
    evens = sorted(range(2, chips, 2), key=lambda m: (m != chips // 2, m))
    return [[m + 1 for m in evens] + [None], evens + [1]]


def in_hbm(x):
    return pltpu.with_memory_space_constraint(x, pltpu.HBM)


def call(kernel, out_shape, operands, scalars=0, scratch=(), megabytes=4, cost=None, in_specs=None):
    several = isinstance(out_shape, (list, tuple))
    specs = [pl.BlockSpec(memory_space=pltpu.SMEM)] * scalars + vmem(len(operands) - scalars)
    return pl.pallas_call(
        kernel,
        out_shape=out_shape,
        in_specs=in_specs or specs,
        out_specs=vmem(len(out_shape)) if several else vmem(1)[0],
        scratch_shapes=list(scratch),
        compiler_params=pltpu.CompilerParams(vmem_limit_bytes=megabytes << 20),
        cost_estimate=cost,
    )(*operands)


def local_gather(
    thinker_rows,
    expert_ids,
    gate_weights,
    w_gate,
    w_up,
    w_down,
    talker_proj,
    talker_slot,
    speech_count,
    left_context,
    frame_offset,
    conv_weight,
):
    devices = lax.axis_size("ep")
    rows, features = thinker_rows.shape
    hidden = w_gate.shape[2]
    talker_width = talker_proj.shape[1]
    horizon = frame_offset.shape[0]
    across = devices // 4
    lists = gather_partners(devices // 2, across)
    back = reduce_partners(devices // 2)
    slots = len(back[0])
    width = -(-3 * devices // LANES) * LANES
    bf16 = functools.partial(jax.ShapeDtypeStruct, dtype=jnp.bfloat16)

    def far(x, chips, j):
        pairs = [(i, i ^ (chips[i % 2][j] * 2)) for i in range(devices) if chips[i % 2][j]]
        return lax.ppermute(x, "ep", pairs)

    def near(x):
        return lax.ppermute(x, "ep", [(i, i ^ 1) for i in range(devices)])

    def both_cores(x):
        return lax.ppermute(x, "ep", [(i, i ^ (2 * across)) for i in range(devices)])

    def side(chips, flip):
        blocks = [[-1, -1] if m is None else [2 * m + flip, 2 * m + 1 - flip] for m in chips]
        return [k for pair in blocks for k in pair]

    def spread(blocks):
        return np.repeat(np.array(blocks, np.int32), rows)

    def arriving(c):
        ours, theirs = lists[c], lists[1 - c]
        blocks = [0, 1, 2 * across, 2 * across + 1]
        blocks += side(ours[:-1], 0) + side(theirs[:-1], 1)
        return spread(blocks + side(ours[-1:], 0) + side(theirs[-1:], 1))

    half = slots // 2
    table = np.stack([arriving(c) for c in range(2)])
    keep_to = np.stack([spread(side(back[c], 0) + [0, 1]) for c in range(2)], axis=1)
    give_to = np.stack([spread(side(back[1 - c], 1)) for c in range(2)], axis=1)
    cut = 2 * rows * half
    target = np.concatenate([give_to, keep_to])

    own = call(
        functools.partial(own_kernel, devices),
        bf16((rows, features + width)),
        [in_hbm(v) for v in (thinker_rows, expert_ids.T, gate_weights.T, talker_slot)],
        megabytes=4,
    )
    other = near(own)
    opposite = both_cores(own)
    pair = call(pair_kernel, bf16((2 * rows, features + width)), [own, other])
    mine = [far(pair, lists, j) for j in range(len(lists[0]))]
    w_up_here, w_down_here = call(
        fetch_kernel,
        [bf16(w_up.shape[1:]), bf16(w_down.shape[1:])],
        [in_hbm(w_up[0]), in_hbm(w_down[0])],
        in_specs=[pl.BlockSpec(memory_space=pltpu.HBM)] * 2,
        scratch=[pltpu.SemaphoreType.DMA((2,))],
        cost=pl.CostEstimate(flops=0, bytes_accessed=4 * w_up.size, transcendentals=0),
    )
    theirs = [near(m) for m in mine]
    early_parts = [pair, opposite, near(opposite)] + mine[:-1] + theirs[:-1]
    early_rows = sum(p.shape[0] for p in early_parts)
    early = call(
        functools.partial(early_kernel, devices),
        bf16((early_rows, hidden)),
        [w_gate[0], w_up_here] + early_parts,
        scratch=[pltpu.VMEM((early_rows, features + width), jnp.bfloat16)],
        megabytes=10,
        cost=pl.CostEstimate(
            flops=4 * early_rows * features * hidden,
            bytes_accessed=4 * w_up.size,
            transcendentals=0,
        ),
    )
    late_parts = [mine[-1], theirs[-1]]
    late_rows = sum(p.shape[0] for p in late_parts)
    parts = early_parts + late_parts
    total = early_rows + late_rows
    give, placed = call(
        functools.partial(late_kernel, devices, rows),
        [bf16((cut, features)), bf16((target.shape[0] - cut, hidden))],
        [table, target, w_gate[0], w_up_here, w_down_here, early] + late_parts,
        scratch=[
            pltpu.VMEM((total, hidden), jnp.bfloat16),
            pltpu.VMEM((late_rows, features + width), jnp.bfloat16),
        ],
        megabytes=12,
    )
    given = [near(give)]
    give, *keep, here = call(
        rest_kernel,
        [bf16((cut, features))] * 3 + [bf16((2 * rows, features))],
        [placed, w_down_here],
        megabytes=6,
        cost=pl.CostEstimate(
            flops=2 * target.shape[0] * features * hidden,
            bytes_accessed=2 * w_down.size,
            transcendentals=0,
        ),
    )
    given.append(near(give))
    chip_sum = []
    for k in range(2):
        chip_sum += call(sum_kernel, [bf16((2 * rows, features))] * half, [keep[k], given[k]])
    arrived = [far(chip_sum[j], back, j) for j in range(slots)]
    context, _ = lax.optimization_barrier((left_context.transpose(1, 0, 2), chip_sum[-1]))
    frames = jax.ShapeDtypeStruct((rows, horizon, talker_width), jnp.float32)
    rest, base, scale = call(
        functools.partial(prepare_kernel, len(parts), rows),
        [bf16((rows, features)), frames, frames],
        [speech_count, table, context, frame_offset, conv_weight] + parts,
        scalars=1,
        scratch=[pltpu.VMEM((total, features), jnp.bfloat16)],
        megabytes=8,
        cost=pl.CostEstimate(
            flops=2 * rows * total * features, bytes_accessed=2 * total * features, transcendentals=0
        ),
    )
    arrived[0], rest, base, scale = lax.optimization_barrier((arrived[0], rest, base, scale))
    partial = here.astype(jnp.float32)
    for a in arrived:
        partial = partial + a.astype(jnp.float32)
    got = near(partial[rows:].astype(jnp.bfloat16))
    return call(
        owner_kernel,
        bf16((rows, horizon, talker_width)),
        [partial, got, rest, talker_proj, base, scale],
        megabytes=8,
    )


def local(thinker_rows, *rest):
    devices = lax.axis_size("ep")
    rows = thinker_rows.shape[0]
    small = rows <= CAP and rows == devices and devices >= 8 and devices & (devices - 1) == 0
    if not small:
        return local_dispatch(thinker_rows, *rest)
    return local_gather(thinker_rows, *rest)


def solution(mesh):
    in_specs = (
        P(("groups", "ep"), None),
        P(("groups", "ep"), None),
        P(("groups", "ep"), None),
        P("ep", None, None),
        P("ep", None, None),
        P("ep", None, None),
        P(),
        P(("groups", "ep"), None),
        P(("groups", "ep")),
        P(("groups", "ep"), None, None),
        P(),
        P(),
    )
    out_specs = P(("groups", "ep"), None, None)
    return jax.shard_map(local, mesh=mesh, in_specs=in_specs, out_specs=out_specs, check_vma=False)
```

```python
import functools

import jax
import jax.numpy as jnp
import numpy as np
from jax import lax
from jax.experimental import pallas as pl
from jax.experimental.pallas import tpu as pltpu
from jax.sharding import PartitionSpec as P


CAP = 16
LANES = 128


def expert_block(block_rows, gate_mat, up_mat, down_mat):
    gate_act = jnp.dot(block_rows, gate_mat, preferred_element_type=jnp.float32)
    up_act = jnp.dot(block_rows, up_mat, preferred_element_type=jnp.float32)
    inner = (jax.nn.silu(gate_act) * up_act).astype(jnp.bfloat16)
    return jnp.dot(inner, down_mat, preferred_element_type=jnp.float32).astype(jnp.bfloat16)


def project(hidden, talker_proj):
    values = hidden.astype(jnp.float32)
    scaled = values * lax.rsqrt(jnp.mean(values * values, axis=-1, keepdims=True) + 1e-06)
    return jnp.dot(
        scaled.astype(jnp.bfloat16), talker_proj, preferred_element_type=jnp.float32
    ).astype(jnp.bfloat16)


def vocode(owned, speech_count, left_context, frame_offset, conv_weight):
    frames = owned.astype(jnp.float32)[:, None, :] + frame_offset[None, :, :]
    sequence = jnp.concatenate([left_context.astype(jnp.float32), frames], axis=1)
    taps = conv_weight.shape[0]
    horizon = frame_offset.shape[0]
    result = jnp.zeros_like(frames)
    for offset in range(taps):
        result = (
            result + conv_weight[offset][None, None, :] * sequence[:, offset : offset + horizon, :]
        )
    active = jnp.arange(horizon, dtype=jnp.int32)[None, :, None] < speech_count[:, None, None]
    return jnp.where(active, result, 0.0).astype(jnp.bfloat16)


def slot_positions(expert_ids, experts):
    flat_expert = expert_ids.reshape(-1)
    onehot = (flat_expert[:, None] == jnp.arange(experts, dtype=jnp.int32)[None, :]).astype(
        jnp.int32
    )
    position = jnp.sum((jnp.cumsum(onehot, axis=0) - onehot) * onehot, axis=1)
    return (flat_expert, position)


def run_and_return(buffer, w_gate, w_up, w_down):
    sources, slot_count, features = buffer.shape
    flattened = buffer.reshape(sources * slot_count, features)
    outputs = expert_block(flattened, w_gate[0], w_up[0], w_down[0]).reshape(
        sources, slot_count, features
    )
    return lax.all_to_all(outputs, "ep", split_axis=0, concat_axis=0, tiled=True)


def local_dispatch(
    thinker_rows,
    expert_ids,
    gate_weights,
    w_gate,
    w_up,
    w_down,
    talker_proj,
    talker_slot,
    speech_count,
    left_context,
    frame_offset,
    conv_weight,
):
    devices = lax.axis_size("ep")
    streams_here, features = thinker_rows.shape
    chosen = expert_ids.shape[1]
    flat_expert, position = slot_positions(expert_ids, devices)
    row_index = jnp.arange(streams_here * chosen, dtype=jnp.int32) // chosen
    outgoing = (
        jnp.zeros((devices, CAP, features), jnp.bfloat16)
        .at[flat_expert, position]
        .set(thinker_rows[row_index])
    )
    returned = run_and_return(
        lax.all_to_all(outgoing, "ep", split_axis=0, concat_axis=0, tiled=True),
        w_gate,
        w_up,
        w_down,
    )
    lookup = (
        returned[flat_expert, position].astype(jnp.float32).reshape(streams_here, chosen, features)
    )
    mixture = jnp.sum(gate_weights[:, :, None] * lookup, axis=1)
    hidden = (thinker_rows.astype(jnp.float32) + mixture).astype(jnp.bfloat16)
    slots = talker_slot[0]
    per_owner = streams_here // devices
    talker_rows = project(hidden, talker_proj)
    placed = (
        jnp.zeros_like(talker_rows)
        .at[slots]
        .set(talker_rows)
        .reshape(devices, per_owner, talker_rows.shape[1])
    )
    owned = lax.all_to_all(placed, "ep", split_axis=0, concat_axis=0, tiled=True).reshape(
        streams_here, talker_rows.shape[1]
    )
    return vocode(owned, speech_count, left_context, frame_offset, conv_weight)


def dot32(a, b):
    return jnp.dot(a, b, preferred_element_type=jnp.float32)


def sort_rows(experts, rows_ref, ids_ref, gates_ref, slot_ref, out_ref, at):
    rows, features = rows_ref.shape
    width = out_ref.shape[1] - features
    owner = lax.broadcasted_iota(jnp.int32, (rows, rows), 0)
    order = (owner == slot_ref[...]).astype(jnp.bfloat16)
    lane = lax.broadcasted_iota(jnp.int32, (width, rows), 0)
    expert = lane % experts
    gates = jnp.zeros((width, rows), jnp.float32)
    for j in range(ids_ref.shape[0]):
        gates = gates + jnp.where(expert == ids_ref[j : j + 1, :], gates_ref[j : j + 1, :], 0.0)
    high = gates.astype(jnp.bfloat16).astype(jnp.float32)
    middle = (gates - high).astype(jnp.bfloat16).astype(jnp.float32)
    low = gates - high - middle
    part = lane // experts
    packed = jnp.where(
        part == 0, high, jnp.where(part == 1, middle, jnp.where(part == 2, low, 0.0))
    ).astype(jnp.bfloat16)
    out_ref[at : at + rows, :features] = dot32(order, rows_ref[...]).astype(jnp.bfloat16)
    out_ref[at : at + rows, features:] = lax.dot_general(
        order, packed, (((1,), (1,)), ((), ())), preferred_element_type=jnp.float32
    ).astype(jnp.bfloat16)


def own_kernel(experts, rows_ref, ids_ref, gates_ref, slot_ref, out_ref):
    sort_rows(experts, rows_ref, ids_ref, gates_ref, slot_ref, out_ref, 0)


def pair_kernel(own_ref, other_ref, out_ref):
    rows = own_ref.shape[0]
    out_ref[:rows, :] = own_ref[...]
    out_ref[rows:, :] = other_ref[...]


def fetch_kernel(*refs):
    count = (len(refs) - 1) // 2
    sems = refs[-1]
    copies = [
        pltpu.make_async_copy(refs[i], refs[count + i], sems.at[i]) for i in range(count)
    ]
    for copy in copies:
        copy.start()
    for copy in copies:
        copy.wait()


def move_rows(me, rows, table_ref, target_ref):
    core = me % 2
    columns = table_ref.shape[1]
    origin = jnp.where(core == 0, table_ref[0:1, :], table_ref[1:2, :])
    owner = lax.broadcasted_iota(jnp.int32, (1, columns), 1) % rows
    target = jnp.where(core == 0, target_ref[:, 0:1], target_ref[:, 1:2])
    rank = lax.broadcasted_iota(jnp.int32, target.shape, 0) % rows
    hit = (origin == (target ^ rank)) & (owner == (target ^ me)) & (target >= 0)
    return jnp.where(hit, 1.0, 0.0).astype(jnp.bfloat16)


def activate(experts, parts, wg_ref, wu_ref, x_ref, inner_ref, first):
    me = lax.axis_index("ep")
    features, hidden = wg_ref.shape
    at = 0
    for part in parts:
        x_ref[at : at + part.shape[0], :] = part[...]
        at += part.shape[0]
    meta = x_ref[:, features:].astype(jnp.float32)
    lane = lax.broadcasted_iota(jnp.int32, (1, meta.shape[1]), 1)
    pick = (lane % experts == me) & (lane < 3 * experts)
    gate = jnp.sum(jnp.where(pick, meta, 0.0), axis=1, keepdims=True)
    step = min(256, hidden)
    for n in range(0, hidden, step):
        g = dot32(x_ref[:, :features], wg_ref[:, n : n + step])
        u = dot32(x_ref[:, :features], wu_ref[:, n : n + step])
        inner = (g * jax.nn.sigmoid(g) * u * gate).astype(jnp.bfloat16)
        inner_ref[first : first + at, n : n + step] = inner


def early_kernel(experts, wg_ref, wu_ref, *refs):
    activate(experts, refs[:-2], wg_ref, wu_ref, refs[-1], refs[-2], 0)


def late_kernel(experts, rows, table_ref, target_ref, wg_ref, wu_ref, wd_ref, early_ref, *refs):
    parts, (out_ref, placed_ref, inner_ref, x_ref) = refs[:-4], refs[-4:]
    first = early_ref.shape[0]
    inner_ref[:first, :] = early_ref[...]
    activate(experts, parts, wg_ref, wu_ref, x_ref, inner_ref, first)
    move = move_rows(lax.axis_index("ep"), rows, table_ref, target_ref)
    placed = dot32(move, inner_ref[...]).astype(jnp.bfloat16)
    cut = out_ref.shape[0]
    placed_ref[...] = placed[cut:]
    down(placed[:cut], wd_ref, [out_ref])


def down(placed, wd_ref, outs):
    features = wd_ref.shape[1]
    step = min(512, features)
    for n in range(0, features, step):
        y = dot32(placed, wd_ref[:, n : n + step]).astype(jnp.bfloat16)
        at = 0
        for out in outs:
            out[:, n : n + step] = y[at : at + out.shape[0]]
            at += out.shape[0]


def rest_kernel(placed_ref, wd_ref, *outs):
    down(placed_ref[...], wd_ref, outs)


def sum_kernel(ours_ref, given_ref, *outs):
    at = 0
    for out in outs:
        piece = slice(at, at + out.shape[0])
        total = ours_ref[piece, :].astype(jnp.float32) + given_ref[piece, :].astype(jnp.float32)
        out[...] = total.astype(jnp.bfloat16)
        at += out.shape[0]


def prepare_kernel(
    blocks, rows, count_ref, table_ref, context_ref, offset_ref, conv_ref, *refs
):
    parts, (rest_ref, base_ref, scale_ref, x_ref) = refs[:blocks], refs[blocks:]
    me = lax.axis_index("ep")
    features = rest_ref.shape[1]
    at = 0
    for part in parts:
        x_ref[at : at + part.shape[0], :] = part[:, :features]
        at += part.shape[0]
    columns = table_ref.shape[1]
    origin = jnp.where(me % 2 == 0, table_ref[0:1, :], table_ref[1:2, :])
    owner = lax.broadcasted_iota(jnp.int32, (1, columns), 1) % rows
    rank = lax.broadcasted_iota(jnp.int32, (rows, 1), 0)
    pick = jnp.where((origin == rank) & (owner == me), 1.0, 0.0).astype(jnp.bfloat16)
    rest_ref[...] = dot32(pick, x_ref[...]).astype(jnp.bfloat16)
    taps, horizon, past = conv_ref.shape[0], offset_ref.shape[0], context_ref.shape[0]
    context = [context_ref[i].astype(jnp.float32) for i in range(past)]
    stream = lax.broadcasted_iota(jnp.int32, (rows, 1), 0)
    count = jnp.zeros((rows, 1), jnp.int32)
    for q in range(rows):
        count = jnp.where(stream == q, count_ref[q], count)
    for f in range(horizon):
        fixed = jnp.zeros((1, conv_ref.shape[1]), jnp.float32)
        scale = jnp.zeros((1, conv_ref.shape[1]), jnp.float32)
        for t in range(past - f, taps):
            i = f + t - past
            fixed = fixed + conv_ref[t : t + 1, :] * offset_ref[i : i + 1, :]
            scale = scale + conv_ref[t : t + 1, :]
        total = jnp.broadcast_to(fixed, context[0].shape)
        for t in range(past - f):
            total = total + conv_ref[t : t + 1, :] * context[f + t]
        base_ref[:, f, :] = jnp.where(f < count, total, 0.0)
        scale_ref[:, f, :] = jnp.where(f < count, jnp.broadcast_to(scale, total.shape), 0.0)


def owner_kernel(mine_ref, got_ref, rest_ref, proj_ref, base_ref, scale_ref, out_ref):
    me = lax.axis_index("ep")
    rows = rest_ref.shape[0]
    total = mine_ref[:rows, :] + got_ref[...].astype(jnp.float32)
    total = total + rest_ref[...].astype(jnp.float32)
    values = total.astype(jnp.bfloat16).astype(jnp.float32)
    normed = values * lax.rsqrt(jnp.mean(values * values, axis=-1, keepdims=True) + 1e-06)
    talker = dot32(normed.astype(jnp.bfloat16), proj_ref[...]).astype(jnp.bfloat16)
    one = lax.broadcasted_iota(jnp.int32, (rows, rows), 0)
    two = lax.broadcasted_iota(jnp.int32, (rows, rows), 1)
    order = jnp.where((one ^ two) == me, 1.0, 0.0).astype(jnp.bfloat16)
    owned = dot32(order, talker)
    for q in range(rows):
        voice = base_ref[q] + scale_ref[q] * owned[q : q + 1, :]
        out_ref[q] = voice.astype(jnp.bfloat16)


def vmem(count):
    return [pl.BlockSpec(memory_space=pltpu.VMEM)] * count


def gather_partners(chips, across):
    others = [m for m in range(1, chips) if m != across]
    middle = len(others) // 2
    order = others[middle - 1 : middle + 1] + others[: middle - 1] + others[: middle : -1]
    return [order[0::2], order[1::2]]


def reduce_partners(chips):
    evens = sorted(range(2, chips, 2), key=lambda m: (m != chips // 2, m))
    last = chips - 2
    ones = [m if m == last else m + 1 for m in evens]
    twos = [m + 1 if m == last else m for m in evens]
    return [ones + [None], twos + [1]]


def in_hbm(x):
    return pltpu.with_memory_space_constraint(x, pltpu.HBM)


def call(kernel, out_shape, operands, scalars=0, scratch=(), megabytes=4, cost=None, in_specs=None):
    several = isinstance(out_shape, (list, tuple))
    specs = [pl.BlockSpec(memory_space=pltpu.SMEM)] * scalars + vmem(len(operands) - scalars)
    return pl.pallas_call(
        kernel,
        out_shape=out_shape,
        in_specs=in_specs or specs,
        out_specs=vmem(len(out_shape)) if several else vmem(1)[0],
        scratch_shapes=list(scratch),
        compiler_params=pltpu.CompilerParams(vmem_limit_bytes=megabytes << 20),
        cost_estimate=cost,
    )(*operands)


def local_gather(
    thinker_rows,
    expert_ids,
    gate_weights,
    w_gate,
    w_up,
    w_down,
    talker_proj,
    talker_slot,
    speech_count,
    left_context,
    frame_offset,
    conv_weight,
):
    devices = lax.axis_size("ep")
    rows, features = thinker_rows.shape
    hidden = w_gate.shape[2]
    talker_width = talker_proj.shape[1]
    horizon = frame_offset.shape[0]
    across = devices // 4
    lists = gather_partners(devices // 2, across)
    back = reduce_partners(devices // 2)
    slots = len(back[0])
    width = -(-3 * devices // LANES) * LANES
    bf16 = functools.partial(jax.ShapeDtypeStruct, dtype=jnp.bfloat16)

    def far(x, chips, j):
        pairs = [(i, i ^ (chips[i % 2][j] * 2)) for i in range(devices) if chips[i % 2][j]]
        return lax.ppermute(x, "ep", pairs)

    def near(x):
        return lax.ppermute(x, "ep", [(i, i ^ 1) for i in range(devices)])

    def both_cores(x):
        return lax.ppermute(x, "ep", [(i, i ^ (2 * across)) for i in range(devices)])

    def side(chips, flip):
        blocks = [[-1, -1] if m is None else [2 * m + flip, 2 * m + 1 - flip] for m in chips]
        return [k for pair in blocks for k in pair]

    def spread(blocks):
        return np.repeat(np.array(blocks, np.int32), rows)

    def arriving(c):
        ours, theirs = lists[c], lists[1 - c]
        blocks = [0, 1, 2 * across, 2 * across + 1]
        blocks += side(ours[:-1], 0) + side(theirs[:-1], 1)
        return spread(blocks + side(ours[-1:], 0) + side(theirs[-1:], 1))

    half = slots // 2
    table = np.stack([arriving(c) for c in range(2)])
    keep_to = np.stack([spread(side(back[c], 0) + [0, 1]) for c in range(2)], axis=1)
    give_to = np.stack([spread(side(back[1 - c], 1)) for c in range(2)], axis=1)
    cut = 2 * rows * half
    target = np.concatenate([give_to, keep_to])

    own = call(
        functools.partial(own_kernel, devices),
        bf16((rows, features + width)),
        [in_hbm(v) for v in (thinker_rows, expert_ids.T, gate_weights.T, talker_slot)],
        megabytes=4,
    )
    other = near(own)
    opposite = both_cores(own)
    pair = call(pair_kernel, bf16((2 * rows, features + width)), [own, other])
    mine = [far(pair, lists, j) for j in range(len(lists[0]))]
    w_up_here, w_down_here = call(
        fetch_kernel,
        [bf16(w_up.shape[1:]), bf16(w_down.shape[1:])],
        [in_hbm(w_up[0]), in_hbm(w_down[0])],
        in_specs=[pl.BlockSpec(memory_space=pltpu.HBM)] * 2,
        scratch=[pltpu.SemaphoreType.DMA((2,))],
        cost=pl.CostEstimate(flops=0, bytes_accessed=4 * w_up.size, transcendentals=0),
    )
    theirs = [near(m) for m in mine]
    early_parts = [pair, opposite, near(opposite)] + mine[:-1] + theirs[:-1]
    early_rows = sum(p.shape[0] for p in early_parts)
    early = call(
        functools.partial(early_kernel, devices),
        bf16((early_rows, hidden)),
        [w_gate[0], w_up_here] + early_parts,
        scratch=[pltpu.VMEM((early_rows, features + width), jnp.bfloat16)],
        megabytes=10,
        cost=pl.CostEstimate(
            flops=4 * early_rows * features * hidden,
            bytes_accessed=4 * w_up.size,
            transcendentals=0,
        ),
    )
    late_parts = [mine[-1], theirs[-1]]
    late_rows = sum(p.shape[0] for p in late_parts)
    parts = early_parts + late_parts
    total = early_rows + late_rows
    give, placed = call(
        functools.partial(late_kernel, devices, rows),
        [bf16((cut, features)), bf16((target.shape[0] - cut, hidden))],
        [table, target, w_gate[0], w_up_here, w_down_here, early] + late_parts,
        scratch=[
            pltpu.VMEM((total, hidden), jnp.bfloat16),
            pltpu.VMEM((late_rows, features + width), jnp.bfloat16),
        ],
        megabytes=12,
    )
    given = [near(give)]
    give, *keep, here = call(
        rest_kernel,
        [bf16((cut, features))] * 3 + [bf16((2 * rows, features))],
        [placed, w_down_here],
        megabytes=6,
        cost=pl.CostEstimate(
            flops=2 * target.shape[0] * features * hidden,
            bytes_accessed=2 * w_down.size,
            transcendentals=0,
        ),
    )
    given.append(near(give))
    chip_sum = []
    for k in range(2):
        chip_sum += call(sum_kernel, [bf16((2 * rows, features))] * half, [keep[k], given[k]])
    arrived = [far(chip_sum[j], back, j) for j in range(slots)]
    context, _ = lax.optimization_barrier((left_context.transpose(1, 0, 2), chip_sum[-1]))
    frames = jax.ShapeDtypeStruct((rows, horizon, talker_width), jnp.float32)
    rest, base, scale = call(
        functools.partial(prepare_kernel, len(parts), rows),
        [bf16((rows, features)), frames, frames],
        [speech_count, table, context, frame_offset, conv_weight] + parts,
        scalars=1,
        scratch=[pltpu.VMEM((total, features), jnp.bfloat16)],
        megabytes=8,
        cost=pl.CostEstimate(
            flops=2 * rows * total * features, bytes_accessed=2 * total * features, transcendentals=0
        ),
    )
    arrived[0], rest, base, scale = lax.optimization_barrier((arrived[0], rest, base, scale))
    partial = here.astype(jnp.float32)
    for a in arrived:
        partial = partial + a.astype(jnp.float32)
    got = near(partial[rows:].astype(jnp.bfloat16))
    return call(
        owner_kernel,
        bf16((rows, horizon, talker_width)),
        [partial, got, rest, talker_proj, base, scale],
        megabytes=8,
    )


def local(thinker_rows, *rest):
    devices = lax.axis_size("ep")
    rows = thinker_rows.shape[0]
    small = rows <= CAP and rows == devices and devices >= 8 and devices & (devices - 1) == 0
    if not small:
        return local_dispatch(thinker_rows, *rest)
    return local_gather(thinker_rows, *rest)


def solution(mesh):
    in_specs = (
        P(("groups", "ep"), None),
        P(("groups", "ep"), None),
        P(("groups", "ep"), None),
        P("ep", None, None),
        P("ep", None, None),
        P("ep", None, None),
        P(),
        P(("groups", "ep"), None),
        P(("groups", "ep")),
        P(("groups", "ep"), None, None),
        P(),
        P(),
    )
    out_specs = P(("groups", "ep"), None, None)
    return jax.shard_map(local, mesh=mesh, in_specs=in_specs, out_specs=out_specs, check_vma=False)
```

```python
import functools

import jax
import jax.numpy as jnp
import numpy as np
from jax import lax
from jax.experimental import pallas as pl
from jax.experimental.pallas import tpu as pltpu
from jax.sharding import PartitionSpec as P


CAP = 16
LANES = 128


def expert_block(block_rows, gate_mat, up_mat, down_mat):
    gate_act = jnp.dot(block_rows, gate_mat, preferred_element_type=jnp.float32)
    up_act = jnp.dot(block_rows, up_mat, preferred_element_type=jnp.float32)
    inner = (jax.nn.silu(gate_act) * up_act).astype(jnp.bfloat16)
    return jnp.dot(inner, down_mat, preferred_element_type=jnp.float32).astype(jnp.bfloat16)


def project(hidden, talker_proj):
    values = hidden.astype(jnp.float32)
    scaled = values * lax.rsqrt(jnp.mean(values * values, axis=-1, keepdims=True) + 1e-06)
    return jnp.dot(
        scaled.astype(jnp.bfloat16), talker_proj, preferred_element_type=jnp.float32
    ).astype(jnp.bfloat16)


def vocode(owned, speech_count, left_context, frame_offset, conv_weight):
    frames = owned.astype(jnp.float32)[:, None, :] + frame_offset[None, :, :]
    sequence = jnp.concatenate([left_context.astype(jnp.float32), frames], axis=1)
    taps = conv_weight.shape[0]
    horizon = frame_offset.shape[0]
    result = jnp.zeros_like(frames)
    for offset in range(taps):
        result = (
            result + conv_weight[offset][None, None, :] * sequence[:, offset : offset + horizon, :]
        )
    active = jnp.arange(horizon, dtype=jnp.int32)[None, :, None] < speech_count[:, None, None]
    return jnp.where(active, result, 0.0).astype(jnp.bfloat16)


def slot_positions(expert_ids, experts):
    flat_expert = expert_ids.reshape(-1)
    onehot = (flat_expert[:, None] == jnp.arange(experts, dtype=jnp.int32)[None, :]).astype(
        jnp.int32
    )
    position = jnp.sum((jnp.cumsum(onehot, axis=0) - onehot) * onehot, axis=1)
    return (flat_expert, position)


def run_and_return(buffer, w_gate, w_up, w_down):
    sources, slot_count, features = buffer.shape
    flattened = buffer.reshape(sources * slot_count, features)
    outputs = expert_block(flattened, w_gate[0], w_up[0], w_down[0]).reshape(
        sources, slot_count, features
    )
    return lax.all_to_all(outputs, "ep", split_axis=0, concat_axis=0, tiled=True)


def local_dispatch(
    thinker_rows,
    expert_ids,
    gate_weights,
    w_gate,
    w_up,
    w_down,
    talker_proj,
    talker_slot,
    speech_count,
    left_context,
    frame_offset,
    conv_weight,
):
    devices = lax.axis_size("ep")
    streams_here, features = thinker_rows.shape
    chosen = expert_ids.shape[1]
    flat_expert, position = slot_positions(expert_ids, devices)
    row_index = jnp.arange(streams_here * chosen, dtype=jnp.int32) // chosen
    outgoing = (
        jnp.zeros((devices, CAP, features), jnp.bfloat16)
        .at[flat_expert, position]
        .set(thinker_rows[row_index])
    )
    returned = run_and_return(
        lax.all_to_all(outgoing, "ep", split_axis=0, concat_axis=0, tiled=True),
        w_gate,
        w_up,
        w_down,
    )
    lookup = (
        returned[flat_expert, position].astype(jnp.float32).reshape(streams_here, chosen, features)
    )
    mixture = jnp.sum(gate_weights[:, :, None] * lookup, axis=1)
    hidden = (thinker_rows.astype(jnp.float32) + mixture).astype(jnp.bfloat16)
    slots = talker_slot[0]
    per_owner = streams_here // devices
    talker_rows = project(hidden, talker_proj)
    placed = (
        jnp.zeros_like(talker_rows)
        .at[slots]
        .set(talker_rows)
        .reshape(devices, per_owner, talker_rows.shape[1])
    )
    owned = lax.all_to_all(placed, "ep", split_axis=0, concat_axis=0, tiled=True).reshape(
        streams_here, talker_rows.shape[1]
    )
    return vocode(owned, speech_count, left_context, frame_offset, conv_weight)


def dot32(a, b):
    return jnp.dot(a, b, preferred_element_type=jnp.float32)


def sort_rows(experts, rows_ref, ids_ref, gates_ref, slot_ref, out_ref, at):
    rows, features = rows_ref.shape
    width = out_ref.shape[1] - features
    owner = lax.broadcasted_iota(jnp.int32, (rows, rows), 0)
    order = (owner == slot_ref[...]).astype(jnp.bfloat16)
    lane = lax.broadcasted_iota(jnp.int32, (width, rows), 0)
    expert = lane % experts
    gates = jnp.zeros((width, rows), jnp.float32)
    for j in range(ids_ref.shape[0]):
        gates = gates + jnp.where(expert == ids_ref[j : j + 1, :], gates_ref[j : j + 1, :], 0.0)
    high = gates.astype(jnp.bfloat16).astype(jnp.float32)
    middle = (gates - high).astype(jnp.bfloat16).astype(jnp.float32)
    low = gates - high - middle
    part = lane // experts
    packed = jnp.where(
        part == 0, high, jnp.where(part == 1, middle, jnp.where(part == 2, low, 0.0))
    ).astype(jnp.bfloat16)
    out_ref[at : at + rows, :features] = dot32(order, rows_ref[...]).astype(jnp.bfloat16)
    out_ref[at : at + rows, features:] = lax.dot_general(
        order, packed, (((1,), (1,)), ((), ())), preferred_element_type=jnp.float32
    ).astype(jnp.bfloat16)


def own_kernel(experts, rows_ref, ids_ref, gates_ref, slot_ref, out_ref):
    sort_rows(experts, rows_ref, ids_ref, gates_ref, slot_ref, out_ref, 0)


def pair_kernel(own_ref, other_ref, out_ref):
    rows = own_ref.shape[0]
    out_ref[:rows, :] = own_ref[...]
    out_ref[rows:, :] = other_ref[...]


def fetch_kernel(*refs):
    count = (len(refs) - 1) // 2
    sems = refs[-1]
    copies = [
        pltpu.make_async_copy(refs[i], refs[count + i], sems.at[i]) for i in range(count)
    ]
    for copy in copies:
        copy.start()
    for copy in copies:
        copy.wait()


def move_rows(me, rows, table_ref, target_ref):
    core = me % 2
    columns = table_ref.shape[1]
    origin = jnp.where(core == 0, table_ref[0:1, :], table_ref[1:2, :])
    owner = lax.broadcasted_iota(jnp.int32, (1, columns), 1) % rows
    target = jnp.where(core == 0, target_ref[:, 0:1], target_ref[:, 1:2])
    rank = lax.broadcasted_iota(jnp.int32, target.shape, 0) % rows
    hit = (origin == (target ^ rank)) & (owner == (target ^ me)) & (target >= 0)
    return jnp.where(hit, 1.0, 0.0).astype(jnp.bfloat16)


def activate(experts, parts, wg_ref, wu_ref, x_ref, inner_ref, first):
    me = lax.axis_index("ep")
    features, hidden = wg_ref.shape
    at = 0
    for part in parts:
        x_ref[at : at + part.shape[0], :] = part[...]
        at += part.shape[0]
    meta = x_ref[:, features:].astype(jnp.float32)
    lane = lax.broadcasted_iota(jnp.int32, (1, meta.shape[1]), 1)
    pick = (lane % experts == me) & (lane < 3 * experts)
    gate = jnp.sum(jnp.where(pick, meta, 0.0), axis=1, keepdims=True)
    step = min(256, hidden)
    for n in range(0, hidden, step):
        g = dot32(x_ref[:, :features], wg_ref[:, n : n + step])
        u = dot32(x_ref[:, :features], wu_ref[:, n : n + step])
        inner = (g * jax.nn.sigmoid(g) * u * gate).astype(jnp.bfloat16)
        inner_ref[first : first + at, n : n + step] = inner


def early_kernel(experts, wg_ref, wu_ref, *refs):
    activate(experts, refs[:-2], wg_ref, wu_ref, refs[-1], refs[-2], 0)


def late_kernel(experts, rows, table_ref, target_ref, wg_ref, wu_ref, wd_ref, early_ref, *refs):
    parts, (out_ref, placed_ref, inner_ref, x_ref) = refs[:-4], refs[-4:]
    first = early_ref.shape[0]
    inner_ref[:first, :] = early_ref[...]
    activate(experts, parts, wg_ref, wu_ref, x_ref, inner_ref, first)
    move = move_rows(lax.axis_index("ep"), rows, table_ref, target_ref)
    placed = dot32(move, inner_ref[...]).astype(jnp.bfloat16)
    cut = out_ref.shape[0]
    placed_ref[...] = placed[cut:]
    down(placed[:cut], wd_ref, [out_ref])


def down(placed, wd_ref, outs):
    features = wd_ref.shape[1]
    step = min(512, features)
    for n in range(0, features, step):
        y = dot32(placed, wd_ref[:, n : n + step]).astype(jnp.bfloat16)
        at = 0
        for out in outs:
            out[:, n : n + step] = y[at : at + out.shape[0]]
            at += out.shape[0]


def rest_kernel(placed_ref, wd_ref, *outs):
    down(placed_ref[...], wd_ref, outs)


def sum_kernel(ours_ref, given_ref, *outs):
    at = 0
    for out in outs:
        piece = slice(at, at + out.shape[0])
        total = ours_ref[piece, :].astype(jnp.float32) + given_ref[piece, :].astype(jnp.float32)
        out[...] = total.astype(jnp.bfloat16)
        at += out.shape[0]


def prepare_kernel(
    blocks, rows, count_ref, table_ref, context_ref, offset_ref, conv_ref, *refs
):
    parts, (rest_ref, base_ref, scale_ref, x_ref) = refs[:blocks], refs[blocks:]
    me = lax.axis_index("ep")
    features = rest_ref.shape[1]
    at = 0
    for part in parts:
        x_ref[at : at + part.shape[0], :] = part[:, :features]
        at += part.shape[0]
    columns = table_ref.shape[1]
    origin = jnp.where(me % 2 == 0, table_ref[0:1, :], table_ref[1:2, :])
    owner = lax.broadcasted_iota(jnp.int32, (1, columns), 1) % rows
    rank = lax.broadcasted_iota(jnp.int32, (rows, 1), 0)
    pick = jnp.where((origin == rank) & (owner == me), 1.0, 0.0).astype(jnp.bfloat16)
    rest_ref[...] = dot32(pick, x_ref[...]).astype(jnp.bfloat16)
    taps, horizon, past = conv_ref.shape[0], offset_ref.shape[0], context_ref.shape[0]
    context = [context_ref[i].astype(jnp.float32) for i in range(past)]
    stream = lax.broadcasted_iota(jnp.int32, (rows, 1), 0)
    count = jnp.zeros((rows, 1), jnp.int32)
    for q in range(rows):
        count = jnp.where(stream == q, count_ref[q], count)
    for f in range(horizon):
        fixed = jnp.zeros((1, conv_ref.shape[1]), jnp.float32)
        scale = jnp.zeros((1, conv_ref.shape[1]), jnp.float32)
        for t in range(past - f, taps):
            i = f + t - past
            fixed = fixed + conv_ref[t : t + 1, :] * offset_ref[i : i + 1, :]
            scale = scale + conv_ref[t : t + 1, :]
        total = jnp.broadcast_to(fixed, context[0].shape)
        for t in range(past - f):
            total = total + conv_ref[t : t + 1, :] * context[f + t]
        base_ref[:, f, :] = jnp.where(f < count, total, 0.0)
        scale_ref[:, f, :] = jnp.where(f < count, jnp.broadcast_to(scale, total.shape), 0.0)


def owner_kernel(mine_ref, got_ref, rest_ref, proj_ref, base_ref, scale_ref, out_ref):
    me = lax.axis_index("ep")
    rows = rest_ref.shape[0]
    total = mine_ref[:rows, :] + got_ref[...].astype(jnp.float32)
    total = total + rest_ref[...].astype(jnp.float32)
    values = total.astype(jnp.bfloat16).astype(jnp.float32)
    normed = values * lax.rsqrt(jnp.mean(values * values, axis=-1, keepdims=True) + 1e-06)
    talker = dot32(normed.astype(jnp.bfloat16), proj_ref[...]).astype(jnp.bfloat16)
    one = lax.broadcasted_iota(jnp.int32, (rows, rows), 0)
    two = lax.broadcasted_iota(jnp.int32, (rows, rows), 1)
    order = jnp.where((one ^ two) == me, 1.0, 0.0).astype(jnp.bfloat16)
    owned = dot32(order, talker)
    for q in range(rows):
        voice = base_ref[q] + scale_ref[q] * owned[q : q + 1, :]
        out_ref[q] = voice.astype(jnp.bfloat16)


def vmem(count):
    return [pl.BlockSpec(memory_space=pltpu.VMEM)] * count


def gather_partners(chips, across):
    others = [m for m in range(1, chips) if m != across]
    middle = len(others) // 2
    order = others[middle - 1 : middle + 1] + others[: middle - 1] + others[: middle : -1]
    return [order[0::2], order[1::2]]


def reduce_partners(chips):
    evens = sorted(range(2, chips, 2), key=lambda m: (m != chips // 2, m))
    last = chips - 2
    ones = [m if m == last else m + 1 for m in evens]
    twos = [m + 1 if m == last else m for m in evens]
    return [ones + [None], twos + [1]]


def in_hbm(x):
    return pltpu.with_memory_space_constraint(x, pltpu.HBM)


def call(kernel, out_shape, operands, scalars=0, scratch=(), megabytes=4, cost=None, in_specs=None):
    several = isinstance(out_shape, (list, tuple))
    specs = [pl.BlockSpec(memory_space=pltpu.SMEM)] * scalars + vmem(len(operands) - scalars)
    return pl.pallas_call(
        kernel,
        out_shape=out_shape,
        in_specs=in_specs or specs,
        out_specs=vmem(len(out_shape)) if several else vmem(1)[0],
        scratch_shapes=list(scratch),
        compiler_params=pltpu.CompilerParams(vmem_limit_bytes=megabytes << 20),
        cost_estimate=cost,
    )(*operands)


def local_gather(
    thinker_rows,
    expert_ids,
    gate_weights,
    w_gate,
    w_up,
    w_down,
    talker_proj,
    talker_slot,
    speech_count,
    left_context,
    frame_offset,
    conv_weight,
):
    devices = lax.axis_size("ep")
    rows, features = thinker_rows.shape
    hidden = w_gate.shape[2]
    talker_width = talker_proj.shape[1]
    horizon = frame_offset.shape[0]
    across = devices // 4
    lists = gather_partners(devices // 2, across)
    back = reduce_partners(devices // 2)
    slots = len(back[0])
    width = -(-3 * devices // LANES) * LANES
    bf16 = functools.partial(jax.ShapeDtypeStruct, dtype=jnp.bfloat16)

    def far(x, chips, j):
        pairs = [(i, i ^ (chips[i % 2][j] * 2)) for i in range(devices) if chips[i % 2][j]]
        return lax.ppermute(x, "ep", pairs)

    def near(x):
        return lax.ppermute(x, "ep", [(i, i ^ 1) for i in range(devices)])

    def both_cores(x):
        return lax.ppermute(x, "ep", [(i, i ^ (2 * across)) for i in range(devices)])

    def side(chips, flip):
        blocks = [[-1, -1] if m is None else [2 * m + flip, 2 * m + 1 - flip] for m in chips]
        return [k for pair in blocks for k in pair]

    def spread(blocks):
        return np.repeat(np.array(blocks, np.int32), rows)

    def arriving(c):
        ours, theirs = lists[c], lists[1 - c]
        blocks = [0, 1, 2 * across, 2 * across + 1]
        blocks += side(ours[:-1], 0) + side(theirs[:-1], 1)
        return spread(blocks + side(ours[-1:], 0) + side(theirs[-1:], 1))

    table = np.stack([arriving(c) for c in range(2)])
    keep_to = np.stack([spread(side(back[c], 0) + [0, 1]) for c in range(2)], axis=1)
    give_to = np.stack([spread(side(back[1 - c], 1)) for c in range(2)], axis=1)
    cut = 2 * rows
    left = cut * (slots - 1)
    target = np.concatenate([give_to, keep_to])

    own = call(
        functools.partial(own_kernel, devices),
        bf16((rows, features + width)),
        [in_hbm(v) for v in (thinker_rows, expert_ids.T, gate_weights.T, talker_slot)],
        megabytes=4,
    )
    other = near(own)
    opposite = both_cores(own)
    pair = call(pair_kernel, bf16((2 * rows, features + width)), [own, other])
    mine = [far(pair, lists, j) for j in range(len(lists[0]))]
    w_up_here, w_down_here = call(
        fetch_kernel,
        [bf16(w_up.shape[1:]), bf16(w_down.shape[1:])],
        [in_hbm(w_up[0]), in_hbm(w_down[0])],
        in_specs=[pl.BlockSpec(memory_space=pltpu.HBM)] * 2,
        scratch=[pltpu.SemaphoreType.DMA((2,))],
        cost=pl.CostEstimate(flops=0, bytes_accessed=4 * w_up.size, transcendentals=0),
    )
    theirs = [near(m) for m in mine]
    early_parts = [pair, opposite, near(opposite)] + mine[:-1] + theirs[:-1]
    early_rows = sum(p.shape[0] for p in early_parts)
    early = call(
        functools.partial(early_kernel, devices),
        bf16((early_rows, hidden)),
        [w_gate[0], w_up_here] + early_parts,
        scratch=[pltpu.VMEM((early_rows, features + width), jnp.bfloat16)],
        megabytes=10,
        cost=pl.CostEstimate(
            flops=4 * early_rows * features * hidden,
            bytes_accessed=4 * w_up.size,
            transcendentals=0,
        ),
    )
    late_parts = [mine[-1], theirs[-1]]
    late_rows = sum(p.shape[0] for p in late_parts)
    parts = early_parts + late_parts
    total = early_rows + late_rows
    give, placed = call(
        functools.partial(late_kernel, devices, rows),
        [bf16((cut, features)), bf16((target.shape[0] - cut, hidden))],
        [table, target, w_gate[0], w_up_here, w_down_here, early] + late_parts,
        scratch=[
            pltpu.VMEM((total, hidden), jnp.bfloat16),
            pltpu.VMEM((late_rows, features + width), jnp.bfloat16),
        ],
        megabytes=12,
    )
    given = [near(give)]
    give, *keep, here = call(
        rest_kernel,
        [bf16((n, features)) for n in (left, cut, left, cut)],
        [placed, w_down_here],
        megabytes=6,
        cost=pl.CostEstimate(
            flops=2 * target.shape[0] * features * hidden,
            bytes_accessed=2 * w_down.size,
            transcendentals=0,
        ),
    )
    given.append(near(give))
    chip_sum = []
    for k in range(2):
        chip_sum += call(
            sum_kernel, [bf16((cut, features))] * (1, slots - 1)[k], [keep[k], given[k]]
        )
    arrived = [far(chip_sum[j], back, j) for j in range(slots)]
    context, _ = lax.optimization_barrier((left_context.transpose(1, 0, 2), chip_sum[-1]))
    frames = jax.ShapeDtypeStruct((rows, horizon, talker_width), jnp.float32)
    rest, base, scale = call(
        functools.partial(prepare_kernel, len(parts), rows),
        [bf16((rows, features)), frames, frames],
        [speech_count, table, context, frame_offset, conv_weight] + parts,
        scalars=1,
        scratch=[pltpu.VMEM((total, features), jnp.bfloat16)],
        megabytes=8,
        cost=pl.CostEstimate(
            flops=2 * rows * total * features, bytes_accessed=2 * total * features, transcendentals=0
        ),
    )
    arrived[0], rest, base, scale = lax.optimization_barrier((arrived[0], rest, base, scale))
    partial = here.astype(jnp.float32)
    for a in arrived:
        partial = partial + a.astype(jnp.float32)
    got = near(partial[rows:].astype(jnp.bfloat16))
    return call(
        owner_kernel,
        bf16((rows, horizon, talker_width)),
        [partial, got, rest, talker_proj, base, scale],
        megabytes=8,
    )


def local(thinker_rows, *rest):
    devices = lax.axis_size("ep")
    rows = thinker_rows.shape[0]
    small = rows <= CAP and rows == devices and devices >= 8 and devices & (devices - 1) == 0
    if not small:
        return local_dispatch(thinker_rows, *rest)
    return local_gather(thinker_rows, *rest)


def solution(mesh):
    in_specs = (
        P(("groups", "ep"), None),
        P(("groups", "ep"), None),
        P(("groups", "ep"), None),
        P("ep", None, None),
        P("ep", None, None),
        P("ep", None, None),
        P(),
        P(("groups", "ep"), None),
        P(("groups", "ep")),
        P(("groups", "ep"), None, None),
        P(),
        P(),
    )
    out_specs = P(("groups", "ep"), None, None)
    return jax.shard_map(local, mesh=mesh, in_specs=in_specs, out_specs=out_specs, check_vma=False)
```
